256 devices in a mesh: pts: 16 (over x, y_lo, core), orb: 16 (over z, y_hi).
Axes of the slice: x: 4, y: 4 (y_hi: 2, y_lo: 2; y = y_hi * 2 + y_lo), z: 8, core: 2. Of those that a mesh axis runs over, the one named last changes fastest.
Arguments:
- amplitudes: float32 [64, 512, 512], P(None, 'orb'), may hold values from -6 to 6
- valence_points: float32 [512, 16384], P('orb', 'pts'), may hold values from -0.4 to 0.4
- conduction_points: float32 [512, 16384], P(None, 'pts'), may hold values from -0.4 to 0.4
- screened: float32 [16384, 16384], P('pts', 'orb'), may hold values from -0.0625 to 0.0625
- valence_energy: float32 [512], P('orb'), may hold values from -1.5 to -0.5
- conduction_energy: float32 [512], replicated, may hold values from 0.5 to 2.5
Outputs:
- second_step: float32 [64, 512, 512], P(None, 'orb')
The draws below stay inside these ranges and needn't reach their ends.
All inputs are finite; a program needn't handle non-finite values.
Results may differ from the reference program's by a relative error of at most 0.000078.
Values sent between devices are 32-bit elements; how exact they have to be, the bound alone decides.
A program may use at most 128 MiB of HBM per device.

```python
import jax
import jax.numpy as jnp
from jax import lax

V = 512
C = 512
P_SIZE = 16384
B = 64


def spiked(values, rng, source, target, blocks, factor):
    def block_of(dim):
        return (jnp.arange(values.shape[dim]) // (values.shape[dim] // blocks)).reshape((-1,) + (1,) * (values.ndim - 1 - dim))

    first = jax.random.permutation(rng, blocks)[block_of(target)]
    second = (block_of(target) + blocks // 2) % blocks
    return jnp.where((block_of(source) == first) | (block_of(source) == second), factor * values, values)


def steps_of(key, extent, cuts, low, high):
    level = 1.0
    for position, blocks in cuts:
        heights = jax.random.uniform(jax.random.fold_in(jax.random.fold_in(key, 6), position), (blocks,), jnp.float32, low / len(cuts), high / len(cuts))
        level = level * jnp.repeat(jnp.exp(heights), extent[position] // blocks).reshape((-1,) + (1,) * (len(extent) - 1 - position))
    return level


def normal_values(stream_key, extent, deviation, most, split=(), dtype=jnp.bfloat16):
    drawn = deviation * jax.random.normal(stream_key, extent, jnp.float32)
    if split:
        drawn = drawn * steps_of(stream_key, extent, split, -0.22, 0.18)
    return jnp.clip(drawn, -most, most).astype(dtype)


def heavy_noise(own_key, dims, scale, reach, cuts, heavy, kind=jnp.bfloat16):
    result = scale * jax.random.normal(own_key, dims, jnp.float32)
    if cuts:
        result = result * steps_of(own_key, dims, cuts, -0.22, 0.18)
    return jnp.clip(spiked(result, jax.random.fold_in(own_key, 3), *heavy), -reach, reach).astype(kind)


def setup_inputs(seed: int = 0) -> dict:
    splits = jax.random.split(jax.random.key(seed), 7)
    return {
        "amplitudes": normal_values(splits[0], (B, V, C), 1.0, 6.0, ((1, 16),), jnp.float32),
        "valence_points": normal_values(splits[1], (V, P_SIZE), 0.0625, 0.4, ((0, 16), (1, 16)), jnp.float32),
        "conduction_points": normal_values(splits[2], (C, P_SIZE), 0.0625, 0.4, ((1, 16),), jnp.float32),
        "screened": heavy_noise(splits[3], (P_SIZE, P_SIZE), P_SIZE ** -0.5, 0.0625, ((0, 16), (1, 16)), (1, 0, 16, 2.0), jnp.float32),
        "valence_energy": jnp.clip(-1.5 + 1.0 * jax.random.uniform(splits[4], (V,), jnp.float32) ** steps_of(splits[4], (V,), ((0, 16),), -0.2, 0.2), -1.5, -0.5),
        "conduction_energy": jnp.clip(jax.random.uniform(splits[5], (C,), jnp.float32, 0.5, 2.5), 0.5, 2.5),
    }


center_shift = 2.5
highest = lax.Precision.HIGHEST


def apply_kernel(block, valence_points, conduction_points, screened):
    def encode_one(vectors):
        prod = jnp.dot(vectors, conduction_points, precision=highest, preferred_element_type=jnp.float32)
        return jnp.sum(prod * valence_points, axis=0)

    encoded = lax.map(encode_one, block)
    interacted = lax.dot_general(encoded, screened, (((1,), (1,)), ((), ())), precision=highest, preferred_element_type=jnp.float32)

    def decode_one(row):
        weighted = valence_points * row[None, :]
        return lax.dot_general(weighted, conduction_points, (((1,), (1,)), ((), ())), precision=highest, preferred_element_type=jnp.float32)

    return lax.map(decode_one, interacted)


def reference(amplitudes, valence_points, conduction_points, screened, valence_energy, conduction_energy):
    energy = conduction_energy[None, :] - valence_energy[:, None]
    kernel_one = apply_kernel(amplitudes, valence_points, conduction_points, screened)
    first_step = 0.5 * (kernel_one + (energy - center_shift) * amplitudes)
    kernel_two = apply_kernel(first_step, valence_points, conduction_points, screened)
    return (kernel_two + (energy - center_shift) * first_step) - amplitudes
```

```python
import functools

import jax
import jax.numpy as jnp
from jax import lax
from jax.experimental import pallas as pl
from jax.experimental.pallas import tpu as pltpu
from jax.sharding import PartitionSpec as P

center_shift = 2.5
precise = lax.Precision.HIGH
MESH = pl.DeviceIdType.MESH
F32 = jnp.float32
BF16 = jnp.bfloat16
ORB = 16
PTS = 16
VMEM = pl.BlockSpec(memory_space=pltpu.VMEM)
ANY = pl.BlockSpec(memory_space=pl.ANY)


def remote(src, dst, send, recv, pts, orb):
    return pltpu.make_async_remote_copy(
        src_ref=src,
        dst_ref=dst,
        send_sem=send,
        recv_sem=recv,
        device_id={"pts": pts, "orb": orb},
        device_id_type=MESH,
    )


def greet(barrier, pts, orb):
    pl.semaphore_signal(barrier, inc=1, device_id={"pts": pts, "orb": orb}, device_id_type=MESH)


def swap_kernel(cp_ref, vp_ref, cp_out, vp_out, send, recv, here):
    p, o = lax.axis_index("pts"), lax.axis_index("orb")
    k = lax.rem(p, 2)
    other = p + 1 - 2 * k
    width = cp_ref.shape[1]
    columns = pl.ds(pl.multiple_of(k * width, width), width)
    barrier = pltpu.get_barrier_semaphore()
    greet(barrier, other, o)
    pl.semaphore_wait(barrier, 1)
    copies = []
    for i, (src, dst) in enumerate(((cp_ref, cp_out), (vp_ref, vp_out))):
        copies.append(remote(src, dst.at[:, columns], send.at[i], recv.at[i], other, o))
        copies.append(pltpu.make_async_copy(src, dst.at[:, columns], here.at[i]))
    for copy in copies:
        copy.start()
    for copy in copies:
        copy.wait()


def swapped(conduction, valence):
    return pl.pallas_call(
        swap_kernel,
        out_shape=(
            jax.ShapeDtypeStruct((conduction.shape[0], 2 * conduction.shape[1]), F32),
            jax.ShapeDtypeStruct((valence.shape[0], 2 * valence.shape[1]), F32),
        ),
        in_specs=[VMEM, VMEM],
        out_specs=(VMEM, VMEM),
        scratch_shapes=[
            pltpu.SemaphoreType.DMA((2,)),
            pltpu.SemaphoreType.DMA((2,)),
            pltpu.SemaphoreType.DMA((2,)),
        ],
        compiler_params=pltpu.CompilerParams(collective_id=0, has_side_effects=True),
        name="swap",
    )(conduction, valence)


def piece_at(ref, row, column):
    return ref.at[pl.ds(pl.multiple_of(row, 8), 8), pl.ds(pl.multiple_of(column, 512), 512)]


def total_of(parts):
    total = parts[0]
    for i in range(1, ORB):
        total = total + parts[i]
    return total


def interact_kernel(
    part_ref, w_ref, out_ref, wbuf, whi, wlo, got1, piece1, chosen, terms, got2, piece2,
    wsem, send1, recv1, send2, recv2, send3, recv3, send4, recv4, here,
):
    p, o = lax.axis_index("pts"), lax.axis_index("orb")
    k = lax.rem(p, 2)
    chip = lax.div(p, 2)
    wcopy = pltpu.make_async_copy(w_ref, wbuf, wsem)
    wcopy.start()

    c4 = lax.rem(o, 4)
    target2 = 2 * chip + lax.div(c4, 2)
    source_chip, source_half = lax.div(o, 2), lax.rem(o, 2)
    self2 = target2 == o
    half4 = lax.div(o, 8)
    self4 = half4 == k

    barrier = pltpu.get_barrier_semaphore()
    for d in range(1, ORB):
        greet(barrier, p, lax.rem(o + d, ORB))
    for j in range(16):
        sp = 2 * source_chip + j // 8
        so = 4 * ((j % 8) // 2) + 2 * source_half + j % 2
        greet(barrier, sp, so)
    for j in range(16):
        greet(barrier, 2 * chip + j // 8, 8 * k + j % 8)
    pl.semaphore_wait(barrier, 15 + 16 + 16)

    sends = []
    for d in range(1, ORB):
        s = lax.rem(o + d, ORB)
        sends.append(
            remote(
                piece_at(part_ref, 8 * lax.div(s, 4), 512 * lax.rem(s, 4)),
                got1.at[o], send1, recv1, p, s,
            )
        )
        sends[-1].start()
    pltpu.make_async_copy(piece_at(part_ref, 8 * lax.div(o, 4), 512 * c4), got1.at[o], recv1).start()

    wcopy.wait()

    def cut(i, carry):
        rows = pl.ds(pl.multiple_of(i * 64, 64), 64)
        value = wbuf[rows, :]
        high = value.astype(BF16)
        whi[rows, :] = high
        wlo[rows, :] = (value - high.astype(F32)).astype(BF16)
        return carry

    lax.fori_loop(0, 16, cut, 0)

    pltpu.make_async_copy(got1, got1, recv1).wait()
    piece1[...] = total_of(got1)

    row2 = 32 * k + 8 * lax.div(o, 4)
    column2 = 512 * lax.rem(c4, 2)
    for d in range(PTS):
        tp = lax.rem(p + d, PTS)
        copy = remote(piece1, piece_at(chosen, row2, column2), send2, recv2, tp, target2)
        if d == 0:
            @pl.when(self2)
            def _():
                pltpu.make_async_copy(piece1, piece_at(chosen, row2, column2), recv2).start()

            @pl.when(jnp.logical_not(self2))
            def _():
                copy.start()
                copy.wait_send()
        else:
            copy.start()
            sends.append(copy)
    pltpu.make_async_copy(chosen, chosen, recv2).wait()

    value = chosen[...]
    high = value.astype(BF16)
    low = (value - high.astype(F32)).astype(BF16)

    def product(a, b):
        return lax.dot_general(a, b, (((1,), (1,)), ((), ())), preferred_element_type=F32)

    for i in range(4):
        rows = slice(256 * i, 256 * i + 256)
        terms[:, rows] = product(high, whi[rows, :]) + (
            product(low, whi[rows, :]) + product(high, wlo[rows, :])
        )

    for d in range(1, ORB):
        s = lax.rem(o + d, ORB)
        sends.append(
            remote(
                piece_at(terms, 8 * lax.div(s, 2), 512 * lax.rem(s, 2)),
                got2.at[o], send3, recv3, p, s,
            )
        )
        sends[-1].start()
    pltpu.make_async_copy(
        piece_at(terms, 8 * lax.div(o, 2), 512 * lax.rem(o, 2)), got2.at[o], recv3
    ).start()
    pltpu.make_async_copy(got2, got2, recv3).wait()
    piece2[...] = total_of(got2)

    row4 = 8 * lax.rem(lax.div(o, 2), 4)
    column4 = 1024 * k + 512 * lax.rem(o, 2)
    tp4 = 2 * chip + half4
    for d in range(ORB):
        copy = remote(piece2, piece_at(out_ref, row4, column4), send4, recv4, tp4, lax.rem(o + d, ORB))
        if d == 0:
            @pl.when(self4)
            def _():
                pltpu.make_async_copy(piece2, piece_at(out_ref, row4, column4), recv4).start()

            @pl.when(jnp.logical_not(self4))
            def _():
                copy.start()
                copy.wait_send()
        else:
            copy.start()
            sends.append(copy)
    pltpu.make_async_copy(out_ref, out_ref, recv4).wait()
    for copy in sends:
        copy.wait_send()


def interacted_of(part, screened):
    dma = pltpu.SemaphoreType.DMA
    return pl.pallas_call(
        interact_kernel,
        out_shape=jax.ShapeDtypeStruct(part.shape, F32),
        in_specs=[VMEM, ANY],
        out_specs=VMEM,
        scratch_shapes=[
            pltpu.VMEM((1024, 1024), F32),
            pltpu.VMEM((1024, 1024), BF16),
            pltpu.VMEM((1024, 1024), BF16),
            pltpu.VMEM((16, 8, 512), F32),
            pltpu.VMEM((8, 512), F32),
            pltpu.VMEM((64, 1024), F32),
            pltpu.VMEM((64, 1024), F32),
            pltpu.VMEM((16, 8, 512), F32),
            pltpu.VMEM((8, 512), F32),
            dma, dma, dma, dma, dma, dma, dma, dma, dma, dma,
        ],
        compiler_params=pltpu.CompilerParams(collective_id=1, has_side_effects=True),
        name="interact",
    )(part, screened)


ROWS = 1024
PARTS = ((0, 40, (0, 1, 2)), (320, 40, (1, 2, 0)), (640, 48, (2, 0, 1)))
CHUNKS = 2
CW = 512 // CHUNKS


def reduce_kernel(scale, final, part_ref, add_ref, out_ref, acc, got, send, recv, *fwd):
    p, o = lax.axis_index("pts"), lax.axis_index("orb")
    k = lax.rem(p, 2)
    x = lax.div(p, 4)
    y = lax.rem(lax.div(p, 2), 2)
    xh, xl = lax.div(x, 2), lax.rem(x, 2)
    coordinate = (lax.rem(xh + xl, 2), xh, y)
    partner = (
        4 * (x + 1 - 2 * xl) + 2 * y + k,
        4 * (3 - x) + 2 * y + k,
        4 * x + 2 * (1 - y) + k,
    )
    mate = p + 1 - 2 * k
    out = out_ref.at[k] if final else out_ref

    barrier = pltpu.get_barrier_semaphore()
    for t in partner:
        greet(barrier, t, o)
    if final:
        greet(barrier, mate, o)
    pl.semaphore_wait(barrier, 4 if final else 3)

    def window(ref, row, count, chunk):
        return ref.at[pl.ds(pl.multiple_of(row, 8), count), pl.ds(chunk * CW, CW)]

    order = [(c, i) for c in range(CHUNKS) for i in range(3)]
    started = []
    base = {}
    got_at, row = {}, 0
    for i, (_, h, _) in enumerate(PARTS):
        for step in range(3):
            got_at[i, step] = row
            row += h * (4 >> step)

    def halve(c, i, step):
        start, h, dims = PARTS[i]
        size = h * (4 >> step)
        lower = start if step == 0 else base[i, step - 1]
        mine = coordinate[dims[step]]
        base[i, step] = lower + mine * size
        source = part_ref if step == 0 else acc
        copy = remote(
            window(source, lower + (1 - mine) * size, size, c),
            window(got, got_at[i, step], size, c),
            send.at[i, step, c], recv.at[i, step, c], partner[dims[step]], o,
        )
        copy.start()
        started.append(copy)
        return copy

    pending = {(c, i): halve(c, i, 0) for c, i in order}
    for step in range(3):
        for c, i in order:
            _, h, dims = PARTS[i]
            size = h * (4 >> step)
            pending[c, i].wait_recv()
            source = part_ref if step == 0 else acc
            summed = window(source, base[i, step], size, c)[...] + window(got, got_at[i, step], size, c)[...]
            if step < 2:
                window(acc, base[i, step], size, c)[...] = summed
                pending[c, i] = halve(c, i, step + 1)
            else:
                window(out, base[i, 2], size, c)[...] = (
                    summed * scale + window(add_ref, base[i, 2], size, c)[...]
                )
                spread_now(out, c, i, 2, base, window, send, recv, partner, o, started, pending)
                if final:
                    forward(out, out_ref, k, base[i, 2], size, c, window, fwd, mate, o, started)
    for step in (2, 1, 0):
        for c, i in order:
            _, h, dims = PARTS[i]
            size = h * (4 >> step)
            pending[c, i].wait_recv()
            if step > 0:
                spread_now(out, c, i, step - 1, base, window, send, recv, partner, o, started, pending)
            if final:
                start, h, dims = PARTS[i]
                lower = start if step == 0 else base[i, step - 1]
                mine = coordinate[dims[step]]
                forward(out, out_ref, k, lower + (1 - mine) * size, size, c, window, fwd, mate, o, started)
    if final:
        fsend, frecv = fwd
        theirs = out_ref.at[1 - k]
        pltpu.make_async_copy(theirs, theirs, frecv).wait()
    for copy in started:
        copy.wait_send()


def spread_now(out, c, i, step, base, window, send, recv, partner, o, started, pending):
    _, h, dims = PARTS[i]
    size = h * (4 >> step)
    block = window(out, base[i, step], size, c)
    copy = remote(block, block, send.at[i, 3 + step, c], recv.at[i, 3 + step, c], partner[dims[step]], o)
    copy.start()
    started.append(copy)
    pending[c, i] = copy


def forward(out, out_ref, k, row, size, c, window, fwd, mate, o, started):
    fsend, frecv = fwd
    block = window(out, row, size, c)
    copy = remote(block, block, fsend, frecv, mate, o)
    copy.start()
    started.append(copy)


def reduced(part, add, scale, final):
    dma = pltpu.SemaphoreType.DMA
    shape = (2, ROWS, 512) if final else (ROWS, 512)
    return pl.pallas_call(
        functools.partial(reduce_kernel, scale, final),
        out_shape=jax.ShapeDtypeStruct(shape, F32),
        in_specs=[VMEM, VMEM],
        out_specs=VMEM,
        scratch_shapes=[
            pltpu.VMEM((ROWS, 512), F32),
            pltpu.VMEM((7 * 128, 512), F32),
            dma((3, 6, CHUNKS)),
            dma((3, 6, CHUNKS)),
            *((dma, dma) if final else ()),
        ],
        compiler_params=pltpu.CompilerParams(
            collective_id=3 if final else 2, has_side_effects=True
        ),
        name="reduce_last" if final else "reduce_first",
    )(part, add)


def encode(block, valence, conduction):
    batch, vrows, cwidth = block.shape
    prod = jnp.dot(
        block.reshape(batch * vrows, cwidth), conduction, precision=precise,
        preferred_element_type=F32,
    )
    return jnp.sum(prod.reshape(batch, vrows, -1) * valence[None], axis=1)


def decode(interacted, valence, conduction):
    weighted = valence[None] * interacted[:, None, :]
    batch, vrows, prows = weighted.shape
    return lax.dot_general(
        weighted.reshape(batch * vrows, prows), conduction, (((1,), (1,)), ((), ())),
        precision=precise, preferred_element_type=F32,
    )


def body(
    amplitudes, valence_points, conduction_points, screened, valence_energy, conduction_energy
):
    k = lax.rem(lax.axis_index("pts"), 2)
    gap = (conduction_energy[None, :] - valence_energy[:, None]) - center_shift
    conduction, valence = swapped(conduction_points, valence_points)
    half = amplitudes.shape[0] // 2
    start = lax.dynamic_slice_in_dim(amplitudes, k * half, half, 0)
    flat = (ROWS, amplitudes.shape[2])

    inter = interacted_of(encode(start, valence, conduction), screened)
    add = (0.5 * gap * start).reshape(flat)
    first = reduced(decode(inter, valence, conduction), add, 0.5, False)
    first = first.reshape(start.shape)

    inter = interacted_of(encode(first, valence, conduction), screened)
    add = (gap * first - start).reshape(flat)
    second = reduced(decode(inter, valence, conduction), add, 1.0, True)
    return second.reshape(amplitudes.shape)


def solution(mesh):
    return jax.shard_map(
        body,
        mesh=mesh,
        in_specs=(
            P(None, "orb", None),
            P("orb", "pts"),
            P(None, "pts"),
            P("pts", "orb"),
            P("orb"),
            P(),
        ),
        out_specs=P(None, "orb", None),
        check_vma=False,
    )
```

```python
import functools

import jax
import jax.numpy as jnp
from jax import lax
from jax.experimental import pallas as pl
from jax.experimental.pallas import tpu as pltpu
from jax.sharding import PartitionSpec as P

center_shift = 2.5
precise = lax.Precision.HIGH
MESH = pl.DeviceIdType.MESH
F32 = jnp.float32
BF16 = jnp.bfloat16
ORB = 16
PTS = 16
VMEM = pl.BlockSpec(memory_space=pltpu.VMEM)
ANY = pl.BlockSpec(memory_space=pl.ANY)


def remote(src, dst, send, recv, pts, orb):
    return pltpu.make_async_remote_copy(
        src_ref=src,
        dst_ref=dst,
        send_sem=send,
        recv_sem=recv,
        device_id={"pts": pts, "orb": orb},
        device_id_type=MESH,
    )


def greet(barrier, pts, orb):
    pl.semaphore_signal(barrier, inc=1, device_id={"pts": pts, "orb": orb}, device_id_type=MESH)


def swap_kernel(cp_ref, vp_ref, cp_out, vp_out, send, recv, here):
    p, o = lax.axis_index("pts"), lax.axis_index("orb")
    k = lax.rem(p, 2)
    other = p + 1 - 2 * k
    width = cp_ref.shape[1]
    columns = pl.ds(pl.multiple_of(k * width, width), width)
    barrier = pltpu.get_barrier_semaphore()
    greet(barrier, other, o)
    pl.semaphore_wait(barrier, 1)
    copies = []
    for i, (src, dst) in enumerate(((cp_ref, cp_out), (vp_ref, vp_out))):
        copies.append(remote(src, dst.at[:, columns], send.at[i], recv.at[i], other, o))
        copies.append(pltpu.make_async_copy(src, dst.at[:, columns], here.at[i]))
    for copy in copies:
        copy.start()
    for copy in copies:
        copy.wait()


def swapped(conduction, valence):
    return pl.pallas_call(
        swap_kernel,
        out_shape=(
            jax.ShapeDtypeStruct((conduction.shape[0], 2 * conduction.shape[1]), F32),
            jax.ShapeDtypeStruct((valence.shape[0], 2 * valence.shape[1]), F32),
        ),
        in_specs=[VMEM, VMEM],
        out_specs=(VMEM, VMEM),
        scratch_shapes=[
            pltpu.SemaphoreType.DMA((2,)),
            pltpu.SemaphoreType.DMA((2,)),
            pltpu.SemaphoreType.DMA((2,)),
        ],
        compiler_params=pltpu.CompilerParams(collective_id=0, has_side_effects=True),
        name="swap",
    )(conduction, valence)


def piece_at(ref, row, column):
    return ref.at[pl.ds(pl.multiple_of(row, 8), 8), pl.ds(pl.multiple_of(column, 512), 512)]


def total_of(parts):
    total = parts[0]
    for i in range(1, ORB):
        total = total + parts[i]
    return total


def interact_kernel(
    part_ref, w_ref, out_ref, wbuf, whi, wlo, got1, got2, piece1, got3, chosen, terms, got4, piece2,
    wsem, send1, recv1, send2, recv2, send3, recv3, send4, recv4, send5, recv5,
):
    p, o = lax.axis_index("pts"), lax.axis_index("orb")
    k = lax.rem(p, 2)
    chip = lax.div(p, 2)
    wcopy = pltpu.make_async_copy(w_ref, wbuf, wsem)
    wcopy.start()

    half5 = lax.div(o, 8)
    self5 = half5 == k

    barrier = pltpu.get_barrier_semaphore()
    for d in range(1, PTS):
        greet(barrier, lax.rem(p + d, PTS), o)
    for d in range(1, ORB):
        greet(barrier, p, lax.rem(o + d, ORB))
    for j in range(16):
        greet(barrier, 2 * chip + j // 8, 8 * k + j % 8)
    pl.semaphore_wait(barrier, 15 + 15 + 16)

    sends = []
    for d in range(PTS):
        t = lax.rem(p + d, PTS)
        for h in range(2):
            source = part_ref.at[
                pl.ds(pl.multiple_of(8 * lax.div(t, 4), 8), 8),
                pl.ds(pl.multiple_of(1024 * h + 256 * lax.rem(t, 4), 256), 256),
            ]
            target = got1.at[2 * chip + h, k]
            if d == 0:
                pltpu.make_async_copy(source, target, recv1).start()
            else:
                sends.append(remote(source, target, send1, recv1, t, o))
                sends[-1].start()

    wcopy.wait()

    def cut(i, carry):
        rows = pl.ds(pl.multiple_of(i * 64, 64), 64)
        value = wbuf[rows, :]
        high = value.astype(BF16)
        whi[rows, :] = high
        wlo[rows, :] = (value - high.astype(F32)).astype(BF16)
        return carry

    lax.fori_loop(0, 16, cut, 0)
    pltpu.make_async_copy(got1, got1, recv1).wait()

    for d in range(ORB):
        s = lax.rem(o + d, ORB)
        if d == 0:
            pltpu.make_async_copy(got1.at[o], got2.at[o], recv2).start()
        else:
            sends.append(remote(got1.at[s], got2.at[o], send2, recv2, p, s))
            sends[-1].start()
    pltpu.make_async_copy(got2, got2, recv2).wait()
    piece1[...] = total_of(got2)

    for d in range(PTS):
        t = lax.rem(p + d, PTS)
        if d == 0:
            pltpu.make_async_copy(piece1, got3.at[p], recv3).start()
        else:
            sends.append(remote(piece1, got3.at[p], send3, recv3, t, o))
            sends[-1].start()
    pltpu.make_async_copy(got3, got3, recv3).wait()
    for t in range(PTS):
        for j in range(2):
            row, column = 32 * j + 8 * (t // 4), 256 * (t % 4)
            chosen[row : row + 8, column : column + 256] = got3[t, j]

    value = chosen[...]
    high = value.astype(BF16)
    low = (value - high.astype(F32)).astype(BF16)

    def product(a, b):
        return lax.dot_general(a, b, (((1,), (1,)), ((), ())), preferred_element_type=F32)

    for i in range(4):
        rows = slice(256 * i, 256 * i + 256)
        terms[:, rows] = product(high, whi[rows, :]) + (
            product(low, whi[rows, :]) + product(high, wlo[rows, :])
        )

    for d in range(1, ORB):
        s = lax.rem(o + d, ORB)
        sends.append(
            remote(
                piece_at(terms, 8 * lax.div(s, 2), 512 * lax.rem(s, 2)),
                got4.at[o], send4, recv4, p, s,
            )
        )
        sends[-1].start()
    pltpu.make_async_copy(
        piece_at(terms, 8 * lax.div(o, 2), 512 * lax.rem(o, 2)), got4.at[o], recv4
    ).start()
    pltpu.make_async_copy(got4, got4, recv4).wait()
    piece2[...] = total_of(got4)

    row5 = 8 * lax.rem(lax.div(o, 2), 4)
    column5 = 1024 * k + 512 * lax.rem(o, 2)
    tp5 = 2 * chip + half5
    for d in range(ORB):
        copy = remote(piece2, piece_at(out_ref, row5, column5), send5, recv5, tp5, lax.rem(o + d, ORB))
        if d == 0:
            @pl.when(self5)
            def _():
                pltpu.make_async_copy(piece2, piece_at(out_ref, row5, column5), recv5).start()

            @pl.when(jnp.logical_not(self5))
            def _():
                copy.start()
                copy.wait_send()
        else:
            copy.start()
            sends.append(copy)
    pltpu.make_async_copy(out_ref, out_ref, recv5).wait()
    for copy in sends:
        copy.wait_send()


def interacted_of(part, screened):
    dma = pltpu.SemaphoreType.DMA
    return pl.pallas_call(
        interact_kernel,
        out_shape=jax.ShapeDtypeStruct(part.shape, F32),
        in_specs=[VMEM, ANY],
        out_specs=VMEM,
        scratch_shapes=[
            pltpu.VMEM((1024, 1024), F32),
            pltpu.VMEM((1024, 1024), BF16),
            pltpu.VMEM((1024, 1024), BF16),
            pltpu.VMEM((16, 2, 8, 256), F32),
            pltpu.VMEM((16, 2, 8, 256), F32),
            pltpu.VMEM((2, 8, 256), F32),
            pltpu.VMEM((16, 2, 8, 256), F32),
            pltpu.VMEM((64, 1024), F32),
            pltpu.VMEM((64, 1024), F32),
            pltpu.VMEM((16, 8, 512), F32),
            pltpu.VMEM((8, 512), F32),
            dma, dma, dma, dma, dma, dma, dma, dma, dma, dma, dma,
        ],
        compiler_params=pltpu.CompilerParams(collective_id=1, has_side_effects=True),
        name="interact",
    )(part, screened)


ROWS = 1024
PARTS = ((0, 40, (0, 1, 2)), (320, 40, (1, 2, 0)), (640, 48, (2, 0, 1)))
CHUNKS = 2
CW = 512 // CHUNKS


def reduce_kernel(scale, final, part_ref, add_ref, out_ref, acc, got, send, recv, *fwd):
    p, o = lax.axis_index("pts"), lax.axis_index("orb")
    k = lax.rem(p, 2)
    x = lax.div(p, 4)
    y = lax.rem(lax.div(p, 2), 2)
    xh, xl = lax.div(x, 2), lax.rem(x, 2)
    coordinate = (lax.rem(xh + xl, 2), xh, y)
    partner = (
        4 * (x + 1 - 2 * xl) + 2 * y + k,
        4 * (3 - x) + 2 * y + k,
        4 * x + 2 * (1 - y) + k,
    )
    mate = p + 1 - 2 * k
    out = out_ref.at[k] if final else out_ref

    barrier = pltpu.get_barrier_semaphore()
    for t in partner:
        greet(barrier, t, o)
    if final:
        greet(barrier, mate, o)
    pl.semaphore_wait(barrier, 4 if final else 3)

    def window(ref, row, count, chunk):
        return ref.at[pl.ds(pl.multiple_of(row, 8), count), pl.ds(chunk * CW, CW)]

    order = [(c, i) for c in range(CHUNKS) for i in range(3)]
    started = []
    base = {}
    got_at, row = {}, 0
    for i, (_, h, _) in enumerate(PARTS):
        for step in range(3):
            got_at[i, step] = row
            row += h * (4 >> step)

    def halve(c, i, step):
        start, h, dims = PARTS[i]
        size = h * (4 >> step)
        lower = start if step == 0 else base[i, step - 1]
        mine = coordinate[dims[step]]
        base[i, step] = lower + mine * size
        source = part_ref if step == 0 else acc
        copy = remote(
            window(source, lower + (1 - mine) * size, size, c),
            window(got, got_at[i, step], size, c),
            send.at[i, step, c], recv.at[i, step, c], partner[dims[step]], o,
        )
        copy.start()
        started.append(copy)
        return copy

    pending = {(c, i): halve(c, i, 0) for c, i in order}
    for step in range(3):
        for c, i in order:
            _, h, dims = PARTS[i]
            size = h * (4 >> step)
            pending[c, i].wait_recv()
            source = part_ref if step == 0 else acc
            summed = window(source, base[i, step], size, c)[...] + window(got, got_at[i, step], size, c)[...]
            if step < 2:
                window(acc, base[i, step], size, c)[...] = summed
                pending[c, i] = halve(c, i, step + 1)
            else:
                window(out, base[i, 2], size, c)[...] = (
                    summed * scale + window(add_ref, base[i, 2], size, c)[...]
                )
                spread_now(out, c, i, 2, base, window, send, recv, partner, o, started, pending)
                if final:
                    forward(out, out_ref, k, base[i, 2], size, c, window, fwd, mate, o, started)
    for step in (2, 1, 0):
        for c, i in order:
            _, h, dims = PARTS[i]
            size = h * (4 >> step)
            pending[c, i].wait_recv()
            if step > 0:
                spread_now(out, c, i, step - 1, base, window, send, recv, partner, o, started, pending)
            if final:
                start, h, dims = PARTS[i]
                lower = start if step == 0 else base[i, step - 1]
                mine = coordinate[dims[step]]
                forward(out, out_ref, k, lower + (1 - mine) * size, size, c, window, fwd, mate, o, started)
    if final:
        fsend, frecv = fwd
        theirs = out_ref.at[1 - k]
        pltpu.make_async_copy(theirs, theirs, frecv).wait()
    for copy in started:
        copy.wait_send()


def spread_now(out, c, i, step, base, window, send, recv, partner, o, started, pending):
    _, h, dims = PARTS[i]
    size = h * (4 >> step)
    block = window(out, base[i, step], size, c)
    copy = remote(block, block, send.at[i, 3 + step, c], recv.at[i, 3 + step, c], partner[dims[step]], o)
    copy.start()
    started.append(copy)
    pending[c, i] = copy


def forward(out, out_ref, k, row, size, c, window, fwd, mate, o, started):
    fsend, frecv = fwd
    block = window(out, row, size, c)
    copy = remote(block, block, fsend, frecv, mate, o)
    copy.start()
    started.append(copy)


def reduced(part, add, scale, final):
    dma = pltpu.SemaphoreType.DMA
    shape = (2, ROWS, 512) if final else (ROWS, 512)
    return pl.pallas_call(
        functools.partial(reduce_kernel, scale, final),
        out_shape=jax.ShapeDtypeStruct(shape, F32),
        in_specs=[VMEM, VMEM],
        out_specs=VMEM,
        scratch_shapes=[
            pltpu.VMEM((ROWS, 512), F32),
            pltpu.VMEM((7 * 128, 512), F32),
            dma((3, 6, CHUNKS)),
            dma((3, 6, CHUNKS)),
            *((dma, dma) if final else ()),
        ],
        compiler_params=pltpu.CompilerParams(
            collective_id=3 if final else 2, has_side_effects=True
        ),
        name="reduce_last" if final else "reduce_first",
    )(part, add)


def encode(block, valence, conduction):
    batch, vrows, cwidth = block.shape
    prod = jnp.dot(
        block.reshape(batch * vrows, cwidth), conduction, precision=precise,
        preferred_element_type=F32,
    )
    return jnp.sum(prod.reshape(batch, vrows, -1) * valence[None], axis=1)


def decode(interacted, valence, conduction):
    weighted = valence[None] * interacted[:, None, :]
    batch, vrows, prows = weighted.shape
    return lax.dot_general(
        weighted.reshape(batch * vrows, prows), conduction, (((1,), (1,)), ((), ())),
        precision=precise, preferred_element_type=F32,
    )


def body(
    amplitudes, valence_points, conduction_points, screened, valence_energy, conduction_energy
):
    k = lax.rem(lax.axis_index("pts"), 2)
    gap = (conduction_energy[None, :] - valence_energy[:, None]) - center_shift
    conduction, valence = swapped(conduction_points, valence_points)
    half = amplitudes.shape[0] // 2
    start = lax.dynamic_slice_in_dim(amplitudes, k * half, half, 0)
    flat = (ROWS, amplitudes.shape[2])

    inter = interacted_of(encode(start, valence, conduction), screened)
    add = (0.5 * gap * start).reshape(flat)
    first = reduced(decode(inter, valence, conduction), add, 0.5, False)
    first = first.reshape(start.shape)

    inter = interacted_of(encode(first, valence, conduction), screened)
    add = (gap * first - start).reshape(flat)
    second = reduced(decode(inter, valence, conduction), add, 1.0, True)
    return second.reshape(amplitudes.shape)


def solution(mesh):
    return jax.shard_map(
        body,
        mesh=mesh,
        in_specs=(
            P(None, "orb", None),
            P("orb", "pts"),
            P(None, "pts"),
            P("pts", "orb"),
            P("orb"),
            P(),
        ),
        out_specs=P(None, "orb", None),
        check_vma=False,
    )
```

```python
import jax
import jax.numpy as jnp
from jax import lax
from jax.experimental import pallas as pl
from jax.experimental.pallas import tpu as pltpu
from jax.sharding import PartitionSpec as P

center_shift = 2.5
MESH = pl.DeviceIdType.MESH
F32 = jnp.float32
BF16 = jnp.bfloat16
ORB = 16
PTS = 16
VMEM = pl.BlockSpec(memory_space=pltpu.VMEM)
ANY = pl.BlockSpec(memory_space=pl.ANY)

ROWS = 1024
CHUNK = 256
CHUNKS = ROWS // CHUNK
UNIT = 64
DIMS = ((0, 1, 2), (1, 2, 0), (2, 0, 1))
SHARES = ((1, 1, 2), (1, 2, 1), (2, 1, 1), (2, 1, 1))


def remote(src, dst, send, recv, pts, orb):
    return pltpu.make_async_remote_copy(
        src_ref=src,
        dst_ref=dst,
        send_sem=send,
        recv_sem=recv,
        device_id={"pts": pts, "orb": orb},
        device_id_type=MESH,
    )


def local(src, dst, sem):
    return pltpu.make_async_copy(src, dst, sem)


def arrived(ref, sem):
    pltpu.make_async_copy(ref, ref, sem).wait()


def greet(barrier, pts, orb):
    pl.semaphore_signal(barrier, inc=1, device_id={"pts": pts, "orb": orb}, device_id_type=MESH)


def two_terms(value):
    high = value.astype(BF16)
    return high, (value - high.astype(F32)).astype(BF16)


def times(a, b, over):
    return lax.dot_general(a, b, (((1,), (over,)), ((), ())), preferred_element_type=F32)


def product(ah, al, bh, bl, over):
    return times(ah, bh, over) + (times(al, bh, over) + times(ah, bl, over))


def total_of(parts):
    total = parts[0]
    for i in range(1, ORB):
        total = total + parts[i]
    return total


def cut_rows(source, high, low, columns=None):
    step = 64

    def cut(i, carry):
        rows = pl.ds(pl.multiple_of(i * step, step), step)
        h, l = two_terms(source[rows, :])
        if columns is None:
            high[rows, :] = h
            low[rows, :] = l
        else:
            high[rows, columns] = h
            low[rows, columns] = l
        return carry

    lax.fori_loop(0, source.shape[0] // step, cut, 0)


def kernel(
    x_hbm, cp_hbm, vp_hbm, w_hbm, gap_ref, out_hbm,
    x, cpown, cpin, ch, cl, vp, wbuf, whi, wlo, part, got1, got2, piece1, got3, chosen, terms,
    got4, piece2, inter, eh, el, dh, dl, kout, acc, got, first, last,
    load, swap_send, swap_recv, flat_send, flat_recv, cube_send, cube_recv, last_sem, mate_send, mate_recv,
):
    p, o = lax.axis_index("pts"), lax.axis_index("orb")
    k = lax.rem(p, 2)
    chip = lax.div(p, 2)
    mate = p + 1 - 2 * k
    own = pl.ds(pl.multiple_of(1024 * k, 1024), 1024)
    other = pl.ds(pl.multiple_of(1024 * (1 - k), 1024), 1024)

    px = lax.div(p, 4)
    py = lax.rem(lax.div(p, 2), 2)
    xh, xl = lax.div(px, 2), lax.rem(px, 2)
    coordinate = (lax.rem(xh + xl, 2), xh, py)
    partner = (
        4 * (px + 1 - 2 * xl) + 2 * py + k,
        4 * (3 - px) + 2 * py + k,
        4 * px + 2 * (1 - py) + k,
    )

    loads = [
        local(cp_hbm, cpown, load.at[0]),
        local(x_hbm.at[pl.ds(pl.multiple_of(ROWS * k, ROWS), ROWS), :], x, load.at[1]),
        local(w_hbm, wbuf, load.at[2]),
        local(vp_hbm, vp.at[:, own], load.at[3]),
    ]
    for copy in loads:
        copy.start()

    barrier = pltpu.get_barrier_semaphore()
    half5 = lax.div(o, 8)
    self5 = half5 == k
    for d in range(1, PTS):
        greet(barrier, lax.rem(p + d, PTS), o)
    for d in range(1, ORB):
        greet(barrier, p, lax.rem(o + d, ORB))
    for j in range(16):
        greet(barrier, 2 * chip + j // 8, 8 * k + j % 8)

    loads[0].wait()
    cut_rows(cpown, ch, cl, own)
    pl.semaphore_wait(barrier, 15 + 15 + 16)

    swaps = [
        remote(cp_hbm, cpin, swap_send.at[0], swap_recv.at[0], mate, o),
        remote(vp_hbm, vp.at[:, own], swap_send.at[1], swap_recv.at[1], mate, o),
    ]
    for copy in swaps:
        copy.start()
    sends = []
    loads[1].wait()
    loads[3].wait()

    def encode_block(source, chunk, app, base, tiles):
        eh[...], el[...] = two_terms(source[chunk * CHUNK : (chunk + 1) * CHUNK, :])

        def tile(n, carry):
            columns = pl.ds(pl.multiple_of(base + 512 * n, 512), 512)
            prod = product(eh[...], el[...], ch[:, columns], cl[:, columns], 0)
            prod = prod.reshape(8, 32, 512) * vp[:, columns][None]
            part[app, 8 * chunk : 8 * chunk + 8, columns] = jnp.sum(prod, axis=1)
            return carry

        lax.fori_loop(0, tiles, tile, 0)

    def decode_block(chunk, app):
        def weigh(j, carry):
            rows = pl.ds(pl.multiple_of(32 * j, 32), 32)
            h, l = two_terms(vp[...] * inter[app, pl.ds(8 * chunk + j, 1), :])
            dh[rows, :] = h
            dl[rows, :] = l
            return carry

        lax.fori_loop(0, 8, weigh, 0)
        kout[app, chunk * CHUNK : (chunk + 1) * CHUNK, :] = product(dh[...], dl[...], ch[...], cl[...], 1)

    def exchange(app):
        sem = lambda i: (flat_send.at[app, i], flat_recv.at[app, i])
        for d in range(PTS):
            t = lax.rem(p + d, PTS)
            for h in range(2):
                source = part.at[
                    app,
                    pl.ds(pl.multiple_of(8 * lax.div(t, 4), 8), 8),
                    pl.ds(pl.multiple_of(1024 * h + 256 * lax.rem(t, 4), 256), 256),
                ]
                target = got1.at[app, 2 * chip + h, k]
                if d == 0:
                    local(source, target, sem(0)[1]).start()
                else:
                    sends.append(remote(source, target, *sem(0), t, o))
                    sends[-1].start()
        if app == 0:
            loads[2].wait()
            cut_rows(wbuf, whi, wlo)
        arrived(got1.at[app], sem(0)[1])

        for d in range(ORB):
            s = lax.rem(o + d, ORB)
            if d == 0:
                local(got1.at[app, o], got2.at[app, o], sem(1)[1]).start()
            else:
                sends.append(remote(got1.at[app, s], got2.at[app, o], *sem(1), p, s))
                sends[-1].start()
        arrived(got2.at[app], sem(1)[1])
        piece1[app] = total_of(got2.at[app])

        for d in range(PTS):
            if d == 0:
                local(piece1.at[app], got3.at[app, p], sem(2)[1]).start()
            else:
                sends.append(remote(piece1.at[app], got3.at[app, p], *sem(2), lax.rem(p + d, PTS), o))
                sends[-1].start()
        arrived(got3.at[app], sem(2)[1])
        for t in range(PTS):
            for j in range(2):
                row, column = 32 * j + 8 * (t // 4), 256 * (t % 4)
                chosen[row : row + 8, column : column + 256] = got3[app, t, j]
        high, low = two_terms(chosen[...])
        for i in range(4):
            rows = slice(256 * i, 256 * i + 256)
            terms[app, :, rows] = product(high, low, whi[rows, :], wlo[rows, :], 1)

        def eighth(s):
            return terms.at[
                app,
                pl.ds(pl.multiple_of(8 * lax.div(s, 2), 8), 8),
                pl.ds(pl.multiple_of(512 * lax.rem(s, 2), 512), 512),
            ]

        for d in range(ORB):
            s = lax.rem(o + d, ORB)
            if d == 0:
                local(eighth(o), got4.at[app, o], sem(3)[1]).start()
            else:
                sends.append(remote(eighth(s), got4.at[app, o], *sem(3), p, s))
                sends[-1].start()
        arrived(got4.at[app], sem(3)[1])
        piece2[app] = total_of(got4.at[app])

        target = inter.at[
            app,
            pl.ds(pl.multiple_of(8 * lax.rem(lax.div(o, 2), 4), 8), 8),
            pl.ds(pl.multiple_of(1024 * k + 512 * lax.rem(o, 2), 512), 512),
        ]
        for d in range(ORB):
            copy = remote(piece2.at[app], target, *sem(4), 2 * chip + half5, lax.rem(o + d, ORB))
            if d == 0:
                @pl.when(self5)
                def _():
                    local(piece2.at[app], target, sem(4)[1]).start()

                @pl.when(jnp.logical_not(self5))
                def _():
                    copy.start()
                    copy.wait_send()
            else:
                copy.start()
                sends.append(copy)
        arrived(inter.at[app], sem(4)[1])

    def decode_and_reduce(app):
        result = last if app else first

        def rows_of(ref, row, count):
            return ref.at[pl.ds(pl.multiple_of(row, 8), count), :]

        base, landing = {}, {}
        row = 0
        for c in range(CHUNKS):
            start = c * CHUNK
            for i in range(3):
                h = 8 * SHARES[c][i]
                lower = start
                for step in range(3):
                    size = h * (4 >> step)
                    base[c, i, step, "lower"] = lower
                    lower = lower + coordinate[DIMS[i][step]] * size
                    base[c, i, step] = lower
                    landing[c, i, step] = row
                    row += size
                start += 8 * h
        flying = {}

        def halve(c, i, step):
            size = 8 * SHARES[c][i] * (4 >> step)
            away = base[c, i, step, "lower"] + (1 - coordinate[DIMS[i][step]]) * size
            flying[c, i] = remote(
                rows_of(acc.at[app] if step else kout.at[app], away, size),
                rows_of(got.at[app], landing[c, i, step], size),
                cube_send.at[app, c, i, step], cube_recv.at[app, c, i, step],
                partner[DIMS[i][step]], o,
            )
            flying[c, i].start()
            sends.append(flying[c, i])

        def spread(c, i, step):
            block = rows_of(result, base[c, i, step], 8 * SHARES[c][i] * (4 >> step))
            flying[c, i] = remote(
                block, block, cube_send.at[app, c, i, 3 + step], cube_recv.at[app, c, i, 3 + step],
                partner[DIMS[i][step]], o,
            )
            flying[c, i].start()
            sends.append(flying[c, i])

        def to_mate(row, size):
            if app:
                copy = remote(
                    rows_of(result, row, size), rows_of(out_hbm.at[k], row, size),
                    mate_send, mate_recv, mate, o,
                )
                copy.start()
                sends.append(copy)

        def advance(c, stage):
            for i in range(3):
                h = 8 * SHARES[c][i]
                if stage == 0:
                    halve(c, i, 0)
                    continue
                flying[c, i].wait_recv()
                if stage <= 3:
                    step = stage - 1
                    size = h * (4 >> step)
                    mine = base[c, i, step]
                    source = acc.at[app] if step else kout.at[app]
                    summed = rows_of(source, mine, size)[...] + rows_of(got.at[app], landing[c, i, step], size)[...]
                    if stage < 3:
                        rows_of(acc.at[app], mine, size)[...] = summed
                        halve(c, i, stage)
                    else:
                        gap = rows_of(gap_ref, lax.rem(mine, 32), h)[...]
                        start = rows_of(x, mine, h)[...]
                        if app:
                            value = (summed + gap * rows_of(first, mine, h)[...]) - start
                        else:
                            value = 0.5 * (summed + gap * start)
                        rows_of(result, mine, h)[...] = value
                        spread(c, i, 2)
                        to_mate(mine, h)
                else:
                    step = 6 - stage
                    size = h * (4 >> step)
                    if step:
                        spread(c, i, step - 1)
                    to_mate(base[c, i, step, "lower"] + (1 - coordinate[DIMS[i][step]]) * size, size)

        for wave in range(CHUNKS + 6):
            for c in reversed(range(CHUNKS)):
                stage = wave - c
                if stage == 0:
                    decode_block(c, app)
                if 0 <= stage <= 6:
                    advance(c, stage)
            c = wave - 6
            if 0 <= c:
                if app:
                    chunk = pl.ds(c * CHUNK, CHUNK)
                    copy = local(last.at[chunk, :], out_hbm.at[k, chunk, :], last_sem.at[c])
                    copy.start()
                    written.append(copy)
                else:
                    encode_block(first, c, 1, 0, 4)

    written = []
    for c in range(CHUNKS):
        encode_block(x, c, 0, 1024 * k, 2)
    for copy in swaps:
        copy.wait_recv()
    cut_rows(cpin, ch, cl, other)
    for c in range(CHUNKS):
        encode_block(x, c, 0, 1024 * (1 - k), 2)
    exchange(0)
    decode_and_reduce(0)
    exchange(1)
    decode_and_reduce(1)
    arrived(out_hbm.at[1 - k], mate_recv)
    for copy in written:
        copy.wait()
    for copy in swaps + sends:
        copy.wait_send()


def steps(amplitudes, conduction, valence, screened, gap):
    dma = pltpu.SemaphoreType.DMA
    f32 = lambda *shape: pltpu.VMEM(shape, F32)
    b16 = lambda *shape: pltpu.VMEM(shape, BF16)
    return pl.pallas_call(
        kernel,
        out_shape=jax.ShapeDtypeStruct((2, ROWS, 512), F32),
        in_specs=[ANY, ANY, ANY, ANY, VMEM],
        out_specs=ANY,
        scratch_shapes=[
            f32(ROWS, 512),
            f32(512, 1024), f32(512, 1024),
            b16(512, 2048), b16(512, 2048),
            f32(32, 2048),
            f32(1024, 1024), b16(1024, 1024), b16(1024, 1024),
            f32(2, 32, 2048),
            f32(2, 16, 2, 8, 256), f32(2, 16, 2, 8, 256), f32(2, 2, 8, 256),
            f32(2, 16, 2, 8, 256), f32(64, 1024), f32(2, 64, 1024),
            f32(2, 16, 8, 512), f32(2, 8, 512), f32(2, 32, 2048),
            b16(CHUNK, 512), b16(CHUNK, 512),
            b16(CHUNK, 2048), b16(CHUNK, 2048),
            f32(2, ROWS, 512), f32(2, ROWS, 512), f32(2, 7 * 128, 512),
            f32(ROWS, 512), f32(ROWS, 512),
            dma((4,)), dma((2,)), dma((2,)), dma((2, 5)), dma((2, 5)),
            dma((2, CHUNKS, 3, 6)), dma((2, CHUNKS, 3, 6)), dma((CHUNKS,)), dma, dma,
        ],
        compiler_params=pltpu.CompilerParams(collective_id=0, has_side_effects=True),
        name="steps",
    )(amplitudes, conduction, valence, screened, gap)


def body(
    amplitudes, valence_points, conduction_points, screened, valence_energy, conduction_energy
):
    gap = (conduction_energy[None, :] - valence_energy[:, None]) - center_shift
    flat = amplitudes.reshape(2 * ROWS, amplitudes.shape[2])
    second = steps(flat, conduction_points, valence_points, screened, gap)
    return second.reshape(amplitudes.shape)


def solution(mesh):
    return jax.shard_map(
        body,
        mesh=mesh,
        in_specs=(
            P(None, "orb", None),
            P("orb", "pts"),
            P(None, "pts"),
            P("pts", "orb"),
            P("orb"),
            P(),
        ),
        out_specs=P(None, "orb", None),
        check_vma=False,
    )
```

```python
import jax
import jax.numpy as jnp
from jax import lax
from jax.experimental import pallas as pl
from jax.experimental.pallas import tpu as pltpu
from jax.sharding import PartitionSpec as P

center_shift = 2.5
MESH = pl.DeviceIdType.MESH
F32 = jnp.float32
BF16 = jnp.bfloat16
ORB = 16
PTS = 16
VMEM = pl.BlockSpec(memory_space=pltpu.VMEM)
ANY = pl.BlockSpec(memory_space=pl.ANY)

ROWS = 1024
CHUNK = 256
CHUNKS = ROWS // CHUNK
UNIT = 64
DIMS = ((0, 1, 2), (1, 2, 0), (2, 0, 1))
SHARES = ((1, 1, 2), (1, 2, 1), (2, 1, 1), (2, 1, 1))


def remote(src, dst, send, recv, pts, orb):
    return pltpu.make_async_remote_copy(
        src_ref=src,
        dst_ref=dst,
        send_sem=send,
        recv_sem=recv,
        device_id={"pts": pts, "orb": orb},
        device_id_type=MESH,
    )


def local(src, dst, sem):
    return pltpu.make_async_copy(src, dst, sem)


def arrived(ref, sem):
    pltpu.make_async_copy(ref, ref, sem).wait()


def greet(barrier, pts, orb):
    pl.semaphore_signal(barrier, inc=1, device_id={"pts": pts, "orb": orb}, device_id_type=MESH)


def two_terms(value):
    high = value.astype(BF16)
    return high, (value - high.astype(F32)).astype(BF16)


def times(a, b, over):
    return lax.dot_general(a, b, (((1,), (over,)), ((), ())), preferred_element_type=F32)


def product(ah, al, bh, bl, over):
    return times(ah, bh, over) + (times(al, bh, over) + times(ah, bl, over))


def total_of(parts):
    total = parts[0]
    for i in range(1, ORB):
        total = total + parts[i]
    return total


def cut_rows(source, high, low, columns=None):
    step = 64

    def cut(i, carry):
        rows = pl.ds(pl.multiple_of(i * step, step), step)
        h, l = two_terms(source[rows, :])
        if columns is None:
            high[rows, :] = h
            low[rows, :] = l
        else:
            high[rows, columns] = h
            low[rows, columns] = l
        return carry

    lax.fori_loop(0, source.shape[0] // step, cut, 0)


def kernel(
    x_hbm, cp_hbm, vp_hbm, w_hbm, gap_ref, out_hbm,
    x, cpown, cpin, ch, cl, vp, wbuf, whi, wlo, part0, part1, got1, got1b, got2, got2b, piece1, piece1b,
    got3, got3b, chosen, terms, got4, piece2, spare, inter, eh, el, dh, dl, kout, acc, got, first, last,
    load, swap_send, swap_recv, flat_send, flat_recv, cube_send, cube_recv, last_sem, mate_send, mate_recv,
):
    p, o = lax.axis_index("pts"), lax.axis_index("orb")
    k = lax.rem(p, 2)
    chip = lax.div(p, 2)
    mate = p + 1 - 2 * k
    own = pl.ds(pl.multiple_of(1024 * k, 1024), 1024)
    other = pl.ds(pl.multiple_of(1024 * (1 - k), 1024), 1024)

    px = lax.div(p, 4)
    py = lax.rem(lax.div(p, 2), 2)
    xh, xl = lax.div(px, 2), lax.rem(px, 2)
    coordinate = (lax.rem(xh + xl, 2), xh, py)
    partner = (
        4 * (px + 1 - 2 * xl) + 2 * py + k,
        4 * (3 - px) + 2 * py + k,
        4 * px + 2 * (1 - py) + k,
    )

    loads = [
        local(cp_hbm, cpown, load.at[0]),
        local(x_hbm, x, load.at[1]),
        local(w_hbm, wbuf, load.at[2]),
        local(vp_hbm, vp.at[:, own], load.at[3]),
    ]
    for i in (0, 3, 1, 2):
        loads[i].start()

    barrier = pltpu.get_barrier_semaphore()
    half5 = lax.div(o, 8)
    self5 = half5 == k
    for d in range(1, PTS):
        greet(barrier, lax.rem(p + d, PTS), o)
    for d in range(1, ORB):
        greet(barrier, p, lax.rem(o + d, ORB))
    for j in range(16):
        greet(barrier, 2 * chip + j // 8, 8 * k + j % 8)

    swaps = [
        remote(cp_hbm, cpin, swap_send.at[0], swap_recv.at[0], mate, o),
        remote(vp_hbm, vp.at[:, own], swap_send.at[1], swap_recv.at[1], mate, o),
    ]
    written = []
    done = set()

    def once(name):
        new = name not in done
        done.add(name)
        return new

    def send(*copy):
        remote(*copy).start()

    def encode_own(half, group):
        row = 1024 * lax.div(group, 2) + 512 * half + 256 * lax.rem(group, 2)
        eh[...], el[...] = two_terms(x[pl.ds(pl.multiple_of(row, 256), 256), :])

        def tile(n, carry):
            columns = pl.ds(pl.multiple_of(1024 * k + 512 * n, 512), 512)
            prod = product(eh[...], el[...], ch[:, columns], cl[:, columns], 0)
            prod = prod.reshape(8, 32, 512) * vp[:, columns][None]
            part0[
                half, pl.ds(pl.multiple_of(8 * group, 8), 8), pl.ds(pl.multiple_of(512 * n, 512), 512)
            ] = jnp.sum(prod, axis=1)
            return carry

        lax.fori_loop(0, 2, tile, 0)

    def encode_chunk(chunk):
        eh[...], el[...] = two_terms(first[chunk * CHUNK : (chunk + 1) * CHUNK, :])

        def tile(n, carry):
            columns = pl.ds(pl.multiple_of(512 * n, 512), 512)
            prod = product(eh[...], el[...], ch[:, columns], cl[:, columns], 0)
            prod = prod.reshape(8, 32, 512) * vp[:, columns][None]
            row = 8 * (chunk % 2)
            part1[chunk // 2, row : row + 8, columns] = jnp.sum(prod, axis=1)
            return carry

        lax.fori_loop(0, 4, tile, 0)

    def decode_chunk(chunk, app):
        def weigh(j, carry):
            rows = pl.ds(pl.multiple_of(32 * j, 32), 32)
            h, l = two_terms(vp[...] * inter[app, chunk // 2, pl.ds(8 * (chunk % 2) + j, 1), :])
            dh[rows, :] = h
            dl[rows, :] = l
            return carry

        lax.fori_loop(0, 8, weigh, 0)
        kout[app, chunk * CHUNK : (chunk + 1) * CHUNK, :] = product(dh[...], dl[...], ch[...], cl[...], 1)

    def exchange(app, half):
        sem = lambda i: (flat_send.at[app, half, i], flat_recv.at[app, half, i])
        g1, g2, g3, one = (
            (r.at[half] for r in ((got1b, got2b, got3b, piece1b) if app else (got1, got2, got3, piece1)))
        )
        if app:
            for d in range(PTS):
                t = lax.rem(p + d, PTS)
                for h in range(2):
                    source = part1.at[
                        half,
                        pl.ds(pl.multiple_of(8 * lax.div(t, 8), 8), 8),
                        pl.ds(pl.multiple_of(1024 * h + 128 * lax.rem(t, 8), 128), 128),
                    ]
                    target = g1.at[2 * chip + h, k]
                    if d == 0:
                        local(source, target, sem(0)[1]).start()
                    else:
                        send(source, target, *sem(0), t, o)
            yield 1.0, 5.0
        else:
            for j in range(4):
                group = lax.rem(px + j, 4)
                encode_own(half, group)
                if once("greeted"):
                    pl.semaphore_wait(barrier, 15 + 15 + 16)
                    for copy in swaps:
                        copy.start()
                for u in range(4):
                    t = 4 * group + lax.rem(p + u, 4)
                    source = part0.at[
                        half,
                        pl.ds(pl.multiple_of(8 * group, 8), 8),
                        pl.ds(pl.multiple_of(256 * lax.rem(p + u, 4), 256), 256),
                    ]
                    if j == 0 and u == 0:
                        local(source, g1.at[p], sem(0)[1]).start()
                    else:
                        send(source, g1.at[p], *sem(0), t, o)
                yield 1.6, 3.0 if j == 3 else 0.0
        arrived(g1, sem(0)[1])

        for d in range(ORB):
            s = lax.rem(o + d, ORB)
            if d == 0:
                local(g1.at[o], g2.at[o], sem(1)[1]).start()
            else:
                send(g1.at[s], g2.at[o], *sem(1), p, s)
        if once("screened"):
            loads[2].wait()
            cut_rows(wbuf, whi, wlo)
        yield 0.8, 7.5
        arrived(g2, sem(1)[1])
        one[...] = total_of(g2)

        for d in range(PTS):
            if d == 0:
                local(one, g3.at[p], sem(2)[1]).start()
            else:
                send(one, g3.at[p], *sem(2), lax.rem(p + d, PTS), o)
        yield 0.8, 5.0
        arrived(g3, sem(2)[1])
        for t in range(PTS):
            if app:
                for j in range(2):
                    row, column = 16 * j + 8 * (t // 8), 128 * (t % 8)
                    chosen[row : row + 8, column : column + 128] = g3[t, j]
            else:
                row, column = 8 * (t // 4), 256 * (t % 4)
                chosen[row : row + 8, column : column + 256] = g3[t]
        high, low = two_terms(chosen[...])
        both = jnp.concatenate([high, low], axis=0)
        assert "screened" in done
        for i in range(4):
            rows = slice(256 * i, 256 * i + 256)
            prod = times(both, whi[rows, :], 1)
            terms[app, half, :, rows] = prod[:32] + (prod[32:] + times(high, wlo[rows, :], 1))

        def share(s):
            return terms.at[
                app, half,
                pl.ds(pl.multiple_of(8 * lax.div(s, 4), 8), 8),
                pl.ds(pl.multiple_of(256 * lax.rem(s, 4), 256), 256),
            ]

        g4, two = got4.at[app, half], piece2.at[app, half]
        for d in range(ORB):
            s = lax.rem(o + d, ORB)
            if d == 0:
                local(share(o), g4.at[o], sem(3)[1]).start()
            else:
                send(share(s), g4.at[o], *sem(3), p, s)
        yield 3.0, 7.5
        arrived(g4, sem(3)[1])
        two[...] = total_of(g4)

        target = inter.at[
            app, half,
            pl.ds(pl.multiple_of(8 * lax.rem(lax.div(o, 4), 2), 8), 8),
            pl.ds(pl.multiple_of(1024 * k + 256 * lax.rem(o, 4), 256), 256),
        ]
        for d in range(ORB):
            copy = remote(two, target, *sem(4), 2 * chip + half5, lax.rem(o + d, ORB))
            if d == 0:
                @pl.when(self5)
                def _():
                    local(two, target, sem(4)[1]).start()
                    local(two, spare.at[app, half], sem(4)[0]).start()

                @pl.when(jnp.logical_not(self5))
                def _():
                    copy.start()
            else:
                copy.start()
        yield 0.8, 7.5
        arrived(inter.at[app, half], sem(4)[1])

    def decode_and_reduce(app, half):
        result = last if app else first
        chunks = (2 * half, 2 * half + 1)

        def rows_of(ref, row, count):
            return ref.at[pl.ds(pl.multiple_of(row, 8), count), :]

        base, landing = {}, {}
        row = 448 * half
        for c in chunks:
            start = c * CHUNK
            for i in range(3):
                h = 8 * SHARES[c][i]
                lower = start
                for step in range(3):
                    size = h * (4 >> step)
                    base[c, i, step, "lower"] = lower
                    lower = lower + coordinate[DIMS[i][step]] * size
                    base[c, i, step] = lower
                    landing[c, i, step] = row
                    row += size
                start += 8 * h
        flying = {}

        def halve(c, i, step):
            size = 8 * SHARES[c][i] * (4 >> step)
            away = base[c, i, step, "lower"] + (1 - coordinate[DIMS[i][step]]) * size
            flying[c, i] = remote(
                rows_of(acc.at[app] if step else kout.at[app], away, size),
                rows_of(got.at[app], landing[c, i, step], size),
                cube_send.at[app, half], cube_recv.at[app, c, i, step],
                partner[DIMS[i][step]], o,
            )
            flying[c, i].start()

        def spread(c, i, step):
            block = rows_of(result, base[c, i, step], 8 * SHARES[c][i] * (4 >> step))
            flying[c, i] = remote(
                block, block, cube_send.at[app, half], cube_recv.at[app, c, i, 3 + step],
                partner[DIMS[i][step]], o,
            )
            flying[c, i].start()

        def to_mate(row, size):
            if app:
                send(rows_of(result, row, size), rows_of(out_hbm.at[k], row, size), mate_send, mate_recv, mate, o)

        def advance(c, stage):
            for i in range(3):
                h = 8 * SHARES[c][i]
                if stage == 0:
                    halve(c, i, 0)
                    continue
                flying[c, i].wait_recv()
                if stage <= 3:
                    step = stage - 1
                    size = h * (4 >> step)
                    mine = base[c, i, step]
                    source = acc.at[app] if step else kout.at[app]
                    summed = rows_of(source, mine, size)[...] + rows_of(got.at[app], landing[c, i, step], size)[...]
                    if stage < 3:
                        rows_of(acc.at[app], mine, size)[...] = summed
                        halve(c, i, stage)
                    else:
                        gap = rows_of(gap_ref, lax.rem(mine, 32), h)[...]
                        start = rows_of(x, ROWS * k + mine, h)[...]
                        if app:
                            value = (summed + gap * rows_of(first, mine, h)[...]) - start
                        else:
                            value = 0.5 * (summed + gap * start)
                        rows_of(result, mine, h)[...] = value
                        spread(c, i, 2)
                        to_mate(mine, h)
                else:
                    step = 6 - stage
                    size = h * (4 >> step)
                    if step:
                        spread(c, i, step - 1)
                    to_mate(base[c, i, step, "lower"] + (1 - coordinate[DIMS[i][step]]) * size, size)

        waves[app, half] = 0
        yield 0.0, 0.0
        if once("swapped"):
            for copy in swaps:
                copy.wait_recv()
            cut_rows(cpin, ch, cl, other)
        for wave in range(2 + 6):
            busy = 0.3
            for c in reversed(chunks):
                stage = wave - (c % 2)
                if stage == 0:
                    decode_chunk(c, app)
                    busy += 2.3
                if 0 <= stage <= 6:
                    advance(c, stage)
            if wave >= 6:
                c = chunks[wave - 6]
                if app:
                    chunk = pl.ds(c * CHUNK, CHUNK)
                    copy = local(last.at[chunk, :], out_hbm.at[k, chunk, :], last_sem.at[c])
                    copy.start()
                    written.append(copy)
                else:
                    encode_chunk(c)
                    busy += 2.8
            waves[app, half] = wave + 1
            yield busy, WAIT[wave]

    def stream(half):
        for app in range(2):
            yield from exchange(app, half)
            yield from decode_and_reduce(app, half)

    for i in (0, 3):
        loads[i].wait()
    cut_rows(cpown, ch, cl, own)
    loads[1].wait()

    waves = {}
    streams = [stream(half) for half in range(2)]
    ready = {0: 0.0, 1: 0.0}
    clock = 0.0

    def held(i):
        if i == 0 or 0 not in ready:
            return False
        return any(
            waves.get((app, 1), 8) < 8 and waves.get((app, 0), -1) < min(waves[app, 1] + LAG, 8)
            for app in range(2)
        )

    while ready:
        half = min(ready, key=lambda i: (held(i), max(ready[i], clock), i))
        clock = max(clock, ready[half])
        try:
            busy, delay = next(streams[half])
        except StopIteration:
            del ready[half]
            continue
        clock += busy
        ready[half] = clock + delay

    arrived(out_hbm.at[1 - k], mate_recv)
    for copy in written:
        copy.wait()
    for copy in swaps:
        copy.wait_send()
    for app in range(2):
        for half in range(2):
            pieces = got4.at[app, half]
            for i in range(4):
                arrived(pieces.at[: ORB - 1], flat_send.at[app, half, i])
            arrived(pieces, flat_send.at[app, half, 4])
            arrived(got.at[app], cube_send.at[app, half])
    arrived(last, mate_send)


LAG = 2
WAIT = (0.0, 1.5, 2.2, 1.8, 1.8, 2.2, 2.5, 0.0)


def steps(amplitudes, conduction, valence, screened, gap):
    dma = pltpu.SemaphoreType.DMA
    f32 = lambda *shape: pltpu.VMEM(shape, F32)
    b16 = lambda *shape: pltpu.VMEM(shape, BF16)
    return pl.pallas_call(
        kernel,
        out_shape=jax.ShapeDtypeStruct((2, ROWS, 512), F32),
        in_specs=[ANY, ANY, ANY, ANY, VMEM],
        out_specs=ANY,
        scratch_shapes=[
            f32(2 * ROWS, 512),
            f32(512, 1024), f32(512, 1024),
            b16(512, 2048), b16(512, 2048),
            f32(32, 2048),
            f32(1024, 1024), b16(1024, 1024), b16(1024, 1024),
            f32(2, 32, 1024), f32(2, 16, 2048),
            f32(2, 16, 8, 256), f32(2, 16, 2, 8, 128),
            f32(2, 16, 8, 256), f32(2, 16, 2, 8, 128),
            f32(2, 8, 256), f32(2, 2, 8, 128),
            f32(2, 16, 8, 256), f32(2, 16, 2, 8, 128),
            f32(32, 1024), f32(2, 2, 32, 1024),
            f32(2, 2, 16, 8, 256), f32(2, 2, 8, 256), f32(2, 2, 8, 256),
            f32(2, 2, 16, 2048),
            b16(CHUNK, 512), b16(CHUNK, 512),
            b16(CHUNK, 2048), b16(CHUNK, 2048),
            f32(2, ROWS, 512), f32(2, ROWS, 512), f32(2, 7 * 128, 512),
            f32(ROWS, 512), f32(ROWS, 512),
            dma((4,)), dma((2,)), dma((2,)), dma((2, 2, 5)), dma((2, 2, 5)),
            dma((2, 2)), dma((2, CHUNKS, 3, 6)), dma((CHUNKS,)), dma, dma,
        ],
        compiler_params=pltpu.CompilerParams(collective_id=0, has_side_effects=True),
        name="steps",
    )(amplitudes, conduction, valence, screened, gap)


def body(
    amplitudes, valence_points, conduction_points, screened, valence_energy, conduction_energy
):
    gap = (conduction_energy[None, :] - valence_energy[:, None]) - center_shift
    flat = amplitudes.reshape(2 * ROWS, amplitudes.shape[2])
    second = steps(flat, conduction_points, valence_points, screened, gap)
    return second.reshape(amplitudes.shape)


def solution(mesh):
    return jax.shard_map(
        body,
        mesh=mesh,
        in_specs=(
            P(None, "orb", None),
            P("orb", "pts"),
            P(None, "pts"),
            P("pts", "orb"),
            P("orb"),
            P(),
        ),
        out_specs=P(None, "orb", None),
        check_vma=False,
    )
```

```python
import jax
import jax.numpy as jnp
from jax import lax
from jax.experimental import pallas as pl
from jax.experimental.pallas import tpu as pltpu
from jax.sharding import PartitionSpec as P

center_shift = 2.5
MESH = pl.DeviceIdType.MESH
F32 = jnp.float32
BF16 = jnp.bfloat16
ORB = 16
PTS = 16
VMEM = pl.BlockSpec(memory_space=pltpu.VMEM)
ANY = pl.BlockSpec(memory_space=pl.ANY)

ROWS = 1024
CHUNK = 256
CHUNKS = ROWS // CHUNK
UNIT = 64
DIMS = ((0, 1, 2), (1, 2, 0), (2, 0, 1))
SHARES = ((1, 1, 2), (1, 2, 1), (2, 1, 1), (2, 1, 1))


def remote(src, dst, send, recv, pts, orb):
    return pltpu.make_async_remote_copy(
        src_ref=src,
        dst_ref=dst,
        send_sem=send,
        recv_sem=recv,
        device_id={"pts": pts, "orb": orb},
        device_id_type=MESH,
    )


def local(src, dst, sem):
    return pltpu.make_async_copy(src, dst, sem)


def arrived(ref, sem):
    pltpu.make_async_copy(ref, ref, sem).wait()


def greet(barrier, pts, orb):
    pl.semaphore_signal(barrier, inc=1, device_id={"pts": pts, "orb": orb}, device_id_type=MESH)


def two_terms(value):
    high = value.astype(BF16)
    return high, (value - high.astype(F32)).astype(BF16)


def times(a, b, over):
    return lax.dot_general(a, b, (((1,), (over,)), ((), ())), preferred_element_type=F32)


def product(ah, al, bh, bl, over):
    return times(ah, bh, over) + (times(al, bh, over) + times(ah, bl, over))


def total_of(parts):
    total = parts[0]
    for i in range(1, ORB):
        total = total + parts[i]
    return total


def cut_rows(source, high, low, columns=None):
    step = 64

    def cut(i, carry):
        rows = pl.ds(pl.multiple_of(i * step, step), step)
        h, l = two_terms(source[rows, :])
        if columns is None:
            high[rows, :] = h
            low[rows, :] = l
        else:
            high[rows, columns] = h
            low[rows, columns] = l
        return carry

    lax.fori_loop(0, source.shape[0] // step, cut, 0)


def kernel(
    x_hbm, cp_hbm, vp_hbm, w_hbm, ve_ref, ce_ref, out_hbm,
    x, cpown, cpin, ch, cl, vp, wbuf, whi, wlo, part0, part1, got1, got1b, got2, got2b, piece1, piece1b,
    got3, got3b, chosen, terms, got4, piece2, spare, inter, eh, el, dh, dl, kout, acc, got, first, last, gap_ref,
    load, swap_send, swap_recv, flat_send, flat_recv, cube_send, cube_recv, last_sem, mate_send, mate_recv,
):
    p, o = lax.axis_index("pts"), lax.axis_index("orb")
    k = lax.rem(p, 2)
    chip = lax.div(p, 2)
    mate = p + 1 - 2 * k
    own = pl.ds(pl.multiple_of(1024 * k, 1024), 1024)
    other = pl.ds(pl.multiple_of(1024 * (1 - k), 1024), 1024)

    px = lax.div(p, 4)
    py = lax.rem(lax.div(p, 2), 2)
    xh, xl = lax.div(px, 2), lax.rem(px, 2)
    coordinate = (lax.rem(xh + xl, 2), xh, py)
    partner = (
        4 * (px + 1 - 2 * xl) + 2 * py + k,
        4 * (3 - px) + 2 * py + k,
        4 * px + 2 * (1 - py) + k,
    )

    loads = [
        local(cp_hbm, cpown, load.at[0]),
        local(x_hbm, x, load.at[1]),
        local(w_hbm, wbuf, load.at[2]),
        local(vp_hbm, vp.at[:, own], load.at[3]),
    ]
    for i in (0, 3, 1, 2):
        loads[i].start()

    barrier = pltpu.get_barrier_semaphore()
    half5 = lax.div(o, 8)
    self5 = half5 == k
    for d in range(1, PTS):
        greet(barrier, lax.rem(p + d, PTS), o)
    for d in range(1, ORB):
        greet(barrier, p, lax.rem(o + d, ORB))
    for j in range(16):
        greet(barrier, 2 * chip + j // 8, 8 * k + j % 8)

    swaps = [
        remote(cp_hbm, cpin, swap_send.at[0], swap_recv.at[0], mate, o),
        remote(vp_hbm, vp.at[:, own], swap_send.at[1], swap_recv.at[1], mate, o),
    ]
    written = []
    done = set()

    def once(name):
        new = name not in done
        done.add(name)
        return new

    def send(*copy):
        remote(*copy).start()

    def encode_own(half, group):
        row = 1024 * lax.div(group, 2) + 512 * half + 256 * lax.rem(group, 2)
        eh[...], el[...] = two_terms(x[pl.ds(pl.multiple_of(row, 256), 256), :])

        def tile(n, carry):
            columns = pl.ds(pl.multiple_of(1024 * k + 512 * n, 512), 512)
            prod = product(eh[...], el[...], ch[:, columns], cl[:, columns], 0)
            prod = prod.reshape(8, 32, 512) * vp[:, columns][None]
            part0[
                half, pl.ds(pl.multiple_of(8 * group, 8), 8), pl.ds(pl.multiple_of(512 * n, 512), 512)
            ] = jnp.sum(prod, axis=1)
            return carry

        lax.fori_loop(0, 2, tile, 0)

    def encode_chunk(chunk):
        eh[...], el[...] = two_terms(first[chunk * CHUNK : (chunk + 1) * CHUNK, :])

        def tile(n, carry):
            columns = pl.ds(pl.multiple_of(512 * n, 512), 512)
            prod = product(eh[...], el[...], ch[:, columns], cl[:, columns], 0)
            prod = prod.reshape(8, 32, 512) * vp[:, columns][None]
            row = 8 * (chunk % 2)
            part1[chunk // 2, row : row + 8, columns] = jnp.sum(prod, axis=1)
            return carry

        lax.fori_loop(0, 4, tile, 0)

    def decode_chunk(chunk, app):
        def weigh(j, carry):
            rows = pl.ds(pl.multiple_of(32 * j, 32), 32)
            h, l = two_terms(vp[...] * inter[app, chunk // 2, pl.ds(8 * (chunk % 2) + j, 1), :])
            dh[rows, :] = h
            dl[rows, :] = l
            return carry

        lax.fori_loop(0, 8, weigh, 0)
        kout[app, chunk * CHUNK : (chunk + 1) * CHUNK, :] = product(dh[...], dl[...], ch[...], cl[...], 1)

    def exchange(app, half):
        sem = lambda i: (flat_send.at[app, half, i], flat_recv.at[app, half, i])
        g1, g2, g3, one = (
            (r.at[half] for r in ((got1b, got2b, got3b, piece1b) if app else (got1, got2, got3, piece1)))
        )
        if app:
            for d in range(PTS):
                t = lax.rem(p + d, PTS)
                for h in range(2):
                    source = part1.at[
                        half,
                        pl.ds(pl.multiple_of(8 * lax.div(t, 8), 8), 8),
                        pl.ds(pl.multiple_of(1024 * h + 128 * lax.rem(t, 8), 128), 128),
                    ]
                    target = g1.at[2 * chip + h, k]
                    if d == 0:
                        local(source, target, sem(0)[1]).start()
                    else:
                        send(source, target, *sem(0), t, o)
            yield 1.0, 5.0
        else:
            for j in range(4):
                group = lax.rem(px + j, 4)
                encode_own(half, group)
                if once("greeted"):
                    pl.semaphore_wait(barrier, 15 + 15 + 16)
                    for copy in swaps:
                        copy.start()
                for u in range(4):
                    t = 4 * group + lax.rem(p + u, 4)
                    source = part0.at[
                        half,
                        pl.ds(pl.multiple_of(8 * group, 8), 8),
                        pl.ds(pl.multiple_of(256 * lax.rem(p + u, 4), 256), 256),
                    ]
                    if j == 0 and u == 0:
                        local(source, g1.at[p], sem(0)[1]).start()
                    else:
                        send(source, g1.at[p], *sem(0), t, o)
                yield 1.6, 3.0 if j == 3 else 0.0
        arrived(g1, sem(0)[1])

        for d in range(ORB):
            s = lax.rem(o + d, ORB)
            if d == 0:
                local(g1.at[o], g2.at[o], sem(1)[1]).start()
            else:
                send(g1.at[s], g2.at[o], *sem(1), p, s)
        if once("screened"):
            loads[2].wait()
            cut_rows(wbuf, whi, wlo)
        yield 0.8, 7.5
        arrived(g2, sem(1)[1])
        one[...] = total_of(g2)

        for d in range(PTS):
            if d == 0:
                local(one, g3.at[p], sem(2)[1]).start()
            else:
                send(one, g3.at[p], *sem(2), lax.rem(p + d, PTS), o)
        yield 0.8, 5.0
        arrived(g3, sem(2)[1])
        for t in range(PTS):
            if app:
                for j in range(2):
                    row, column = 16 * j + 8 * (t // 8), 128 * (t % 8)
                    chosen[row : row + 8, column : column + 128] = g3[t, j]
            else:
                row, column = 8 * (t // 4), 256 * (t % 4)
                chosen[row : row + 8, column : column + 256] = g3[t]
        high, low = two_terms(chosen[...])
        both = jnp.concatenate([high, low], axis=0)
        assert "screened" in done
        for i in range(4):
            rows = slice(256 * i, 256 * i + 256)
            prod = times(both, whi[rows, :], 1)
            terms[app, half, :, rows] = prod[:32] + (prod[32:] + times(high, wlo[rows, :], 1))

        def share(s):
            return terms.at[
                app, half,
                pl.ds(pl.multiple_of(8 * lax.div(s, 4), 8), 8),
                pl.ds(pl.multiple_of(256 * lax.rem(s, 4), 256), 256),
            ]

        g4, two = got4.at[app, half], piece2.at[app, half]
        for d in range(ORB):
            s = lax.rem(o + d, ORB)
            if d == 0:
                local(share(o), g4.at[o], sem(3)[1]).start()
            else:
                send(share(s), g4.at[o], *sem(3), p, s)
        yield 3.0, 7.5
        arrived(g4, sem(3)[1])
        two[...] = total_of(g4)

        target = inter.at[
            app, half,
            pl.ds(pl.multiple_of(8 * lax.rem(lax.div(o, 4), 2), 8), 8),
            pl.ds(pl.multiple_of(1024 * k + 256 * lax.rem(o, 4), 256), 256),
        ]
        for d in range(ORB):
            copy = remote(two, target, *sem(4), 2 * chip + half5, lax.rem(o + d, ORB))
            if d == 0:
                @pl.when(self5)
                def _():
                    local(two, target, sem(4)[1]).start()
                    local(two, spare.at[app, half], sem(4)[0]).start()

                @pl.when(jnp.logical_not(self5))
                def _():
                    copy.start()
            else:
                copy.start()
        yield 0.8, 7.5
        arrived(inter.at[app, half], sem(4)[1])

    def decode_and_reduce(app, half):
        result = last if app else first
        chunks = (2 * half, 2 * half + 1)

        def rows_of(ref, row, count):
            return ref.at[pl.ds(pl.multiple_of(row, 8), count), :]

        base, landing = {}, {}
        row = 448 * half
        for c in chunks:
            start = c * CHUNK
            for i in range(3):
                h = 8 * SHARES[c][i]
                lower = start
                for step in range(3):
                    size = h * (4 >> step)
                    base[c, i, step, "lower"] = lower
                    lower = lower + coordinate[DIMS[i][step]] * size
                    base[c, i, step] = lower
                    landing[c, i, step] = row
                    row += size
                start += 8 * h
        flying = {}

        def halve(c, i, step):
            size = 8 * SHARES[c][i] * (4 >> step)
            away = base[c, i, step, "lower"] + (1 - coordinate[DIMS[i][step]]) * size
            flying[c, i] = remote(
                rows_of(acc.at[app] if step else kout.at[app], away, size),
                rows_of(got.at[app], landing[c, i, step], size),
                cube_send.at[app, half], cube_recv.at[app, c, i, step],
                partner[DIMS[i][step]], o,
            )
            flying[c, i].start()

        def spread(c, i, step):
            block = rows_of(result, base[c, i, step], 8 * SHARES[c][i] * (4 >> step))
            flying[c, i] = remote(
                block, block, cube_send.at[app, half], cube_recv.at[app, c, i, 3 + step],
                partner[DIMS[i][step]], o,
            )
            flying[c, i].start()

        def to_mate(row, size):
            if app:
                send(rows_of(result, row, size), rows_of(out_hbm.at[k], row, size), mate_send, mate_recv, mate, o)

        def advance(c, stage):
            for i in range(3):
                h = 8 * SHARES[c][i]
                if stage == 0:
                    halve(c, i, 0)
                    continue
                flying[c, i].wait_recv()
                if stage <= 3:
                    step = stage - 1
                    size = h * (4 >> step)
                    mine = base[c, i, step]
                    source = acc.at[app] if step else kout.at[app]
                    summed = rows_of(source, mine, size)[...] + rows_of(got.at[app], landing[c, i, step], size)[...]
                    if stage < 3:
                        rows_of(acc.at[app], mine, size)[...] = summed
                        halve(c, i, stage)
                    else:
                        gap = rows_of(gap_ref, lax.rem(mine, 32), h)[...]
                        start = rows_of(x, ROWS * k + mine, h)[...]
                        if app:
                            value = (summed + gap * rows_of(first, mine, h)[...]) - start
                        else:
                            value = 0.5 * (summed + gap * start)
                        rows_of(result, mine, h)[...] = value
                        spread(c, i, 2)
                        to_mate(mine, h)
                else:
                    step = 6 - stage
                    size = h * (4 >> step)
                    if step:
                        spread(c, i, step - 1)
                    to_mate(base[c, i, step, "lower"] + (1 - coordinate[DIMS[i][step]]) * size, size)

        if once("swapped"):
            for copy in swaps:
                copy.wait_recv()
            cut_rows(cpin, ch, cl, other)
        for wave in range(2 + 6):
            busy = 0.3
            for c in reversed(chunks):
                stage = wave - (c % 2)
                if stage == 0:
                    decode_chunk(c, app)
                    busy += 2.3
                if 0 <= stage <= 6:
                    advance(c, stage)
            if wave >= 6:
                c = chunks[wave - 6]
                if app:
                    chunk = pl.ds(c * CHUNK, CHUNK)
                    copy = local(last.at[chunk, :], out_hbm.at[k, chunk, :], last_sem.at[c])
                    copy.start()
                    written.append(copy)
                else:
                    encode_chunk(c)
                    busy += 2.8
            yield busy, (0.0 if wave in (0, 7) else WAIT[wave])

    def stream(half):
        for app in range(2):
            yield from exchange(app, half)
            yield from decode_and_reduce(app, half)

    for v in range(32):
        gap_ref[v : v + 1, :] = (ce_ref[...] - ve_ref[v]) - center_shift
    for i in (0, 3):
        loads[i].wait()
    cut_rows(cpown, ch, cl, own)
    loads[1].wait()

    streams = [stream(half) for half in range(2)]
    ready = {0: 0.0, 1: 0.0}
    clock = 0.0
    while ready:
        half = min(ready, key=lambda i: (max(ready[i], clock), i))
        clock = max(clock, ready[half])
        try:
            busy, delay = next(streams[half])
        except StopIteration:
            del ready[half]
            continue
        clock += busy
        ready[half] = clock + delay

    arrived(out_hbm.at[1 - k], mate_recv)
    for copy in written:
        copy.wait()
    for copy in swaps:
        copy.wait_send()
    for app in range(2):
        for half in range(2):
            pieces = got4.at[app, half]
            for i in range(4):
                arrived(pieces.at[: ORB - 1], flat_send.at[app, half, i])
            arrived(pieces, flat_send.at[app, half, 4])
            arrived(got.at[app], cube_send.at[app, half])
    arrived(last, mate_send)


WAIT = (0.0, 3.0, 2.5, 2.0, 2.0, 2.5, 3.0, 0.0)


def steps(amplitudes, conduction, valence, screened, lower, upper):
    dma = pltpu.SemaphoreType.DMA
    f32 = lambda *shape: pltpu.VMEM(shape, F32)
    b16 = lambda *shape: pltpu.VMEM(shape, BF16)
    return pl.pallas_call(
        kernel,
        out_shape=jax.ShapeDtypeStruct((2, ROWS, 512), F32),
        in_specs=[ANY, ANY, ANY, ANY, pl.BlockSpec(memory_space=pltpu.SMEM), VMEM],
        out_specs=ANY,
        scratch_shapes=[
            f32(2 * ROWS, 512),
            f32(512, 1024), f32(512, 1024),
            b16(512, 2048), b16(512, 2048),
            f32(32, 2048),
            f32(1024, 1024), b16(1024, 1024), b16(1024, 1024),
            f32(2, 32, 1024), f32(2, 16, 2048),
            f32(2, 16, 8, 256), f32(2, 16, 2, 8, 128),
            f32(2, 16, 8, 256), f32(2, 16, 2, 8, 128),
            f32(2, 8, 256), f32(2, 2, 8, 128),
            f32(2, 16, 8, 256), f32(2, 16, 2, 8, 128),
            f32(32, 1024), f32(2, 2, 32, 1024),
            f32(2, 2, 16, 8, 256), f32(2, 2, 8, 256), f32(2, 2, 8, 256),
            f32(2, 2, 16, 2048),
            b16(CHUNK, 512), b16(CHUNK, 512),
            b16(CHUNK, 2048), b16(CHUNK, 2048),
            f32(2, ROWS, 512), f32(2, ROWS, 512), f32(2, 7 * 128, 512),
            f32(ROWS, 512), f32(ROWS, 512), f32(32, 512),
            dma((4,)), dma((2,)), dma((2,)), dma((2, 2, 5)), dma((2, 2, 5)),
            dma((2, 2)), dma((2, CHUNKS, 3, 6)), dma((CHUNKS,)), dma, dma,
        ],
        compiler_params=pltpu.CompilerParams(collective_id=0, has_side_effects=True),
        name="steps",
    )(amplitudes, conduction, valence, screened, lower, upper)


def body(
    amplitudes, valence_points, conduction_points, screened, valence_energy, conduction_energy
):
    flat = amplitudes.reshape(2 * ROWS, amplitudes.shape[2])
    second = steps(
        flat, conduction_points, valence_points, screened, valence_energy, conduction_energy[None, :]
    )
    return second.reshape(amplitudes.shape)


def solution(mesh):
    return jax.shard_map(
        body,
        mesh=mesh,
        in_specs=(
            P(None, "orb", None),
            P("orb", "pts"),
            P(None, "pts"),
            P("pts", "orb"),
            P("orb"),
            P(),
        ),
        out_specs=P(None, "orb", None),
        check_vma=False,
    )
```

```python
import jax
import jax.numpy as jnp
from jax import lax
from jax.experimental import pallas as pl
from jax.experimental.pallas import tpu as pltpu
from jax.sharding import PartitionSpec as P

center_shift = 2.5
MESH = pl.DeviceIdType.MESH
F32 = jnp.float32
BF16 = jnp.bfloat16
ORB = 16
PTS = 16
VMEM = pl.BlockSpec(memory_space=pltpu.VMEM)
ANY = pl.BlockSpec(memory_space=pl.ANY)

ROWS = 1024
CHUNK = 256
CHUNKS = ROWS // CHUNK
FARTHEST = (8, 7, 9, 6, 10, 5, 11, 4, 12, 3, 13, 2, 14, 1, 15, 0)
DIMS = ((0, 1, 2), (1, 2, 0), (2, 0, 1))
SHARES = ((1, 1, 2), (1, 2, 1), (2, 1, 1), (2, 1, 1))


def remote(src, dst, send, recv, pts, orb):
    return pltpu.make_async_remote_copy(
        src_ref=src,
        dst_ref=dst,
        send_sem=send,
        recv_sem=recv,
        device_id={"pts": pts, "orb": orb},
        device_id_type=MESH,
    )


def local(src, dst, sem):
    return pltpu.make_async_copy(src, dst, sem)


def arrived(ref, sem):
    pltpu.make_async_copy(ref, ref, sem).wait()


def greet(barrier, pts, orb):
    pl.semaphore_signal(barrier, inc=1, device_id={"pts": pts, "orb": orb}, device_id_type=MESH)


def two_terms(value):
    high = value.astype(BF16)
    return high, (value - high.astype(F32)).astype(BF16)


def times(a, b, over):
    return lax.dot_general(a, b, (((1,), (over,)), ((), ())), preferred_element_type=F32)


def product(ah, al, bh, bl, over):
    return times(ah, bh, over) + (times(al, bh, over) + times(ah, bl, over))


def total_of(parts):
    total = parts[0]
    for i in range(1, ORB):
        total = total + parts[i]
    return total


def cut_rows(source, high, low, columns=None):
    step = 64

    def cut(i, carry):
        rows = pl.ds(pl.multiple_of(i * step, step), step)
        h, l = two_terms(source[rows, :])
        if columns is None:
            high[rows, :] = h
            low[rows, :] = l
        else:
            high[rows, columns] = h
            low[rows, columns] = l
        return carry

    lax.fori_loop(0, source.shape[0] // step, cut, 0)


def kernel(
    x_hbm, cp_hbm, vp_hbm, w_hbm, ve_ref, ce_ref, out_hbm,
    x, cpown, cpin, ch, cl, vp, wbuf, whi, wlo, part0, part1, got1, got1b, got2, got2b, piece1, piece1b,
    got3, got3b, chosen, terms, got4, piece2, spare, inter, eh, el, dh, dl, kout, acc, got, first, last, gap_ref,
    load, swap_send, swap_recv, flat_send, flat_recv, cube_send, cube_recv, last_sem, mate_send, mate_recv,
):
    p, o = lax.axis_index("pts"), lax.axis_index("orb")
    k = lax.rem(p, 2)
    chip = lax.div(p, 2)
    mate = p + 1 - 2 * k
    own = pl.ds(pl.multiple_of(1024 * k, 1024), 1024)
    other = pl.ds(pl.multiple_of(1024 * (1 - k), 1024), 1024)

    px = lax.div(p, 4)
    py = lax.rem(lax.div(p, 2), 2)
    xh, xl = lax.div(px, 2), lax.rem(px, 2)
    coordinate = (lax.rem(xh + xl, 2), xh, py)
    partner = (
        4 * (px + 1 - 2 * xl) + 2 * py + k,
        4 * (3 - px) + 2 * py + k,
        4 * px + 2 * (1 - py) + k,
    )

    loads = [
        local(cp_hbm, cpown, load.at[0]),
        local(x_hbm, x, load.at[1]),
        local(w_hbm, wbuf, load.at[2]),
        local(vp_hbm, vp.at[:, own], load.at[3]),
    ]
    for i in (0, 3, 1, 2):
        loads[i].start()

    barrier = pltpu.get_barrier_semaphore()
    half5 = lax.div(o, 8)
    self5 = half5 == k
    for d in range(1, PTS):
        greet(barrier, lax.rem(p + d, PTS), o)
    for d in range(1, ORB):
        greet(barrier, p, lax.rem(o + d, ORB))
    for j in range(16):
        greet(barrier, 2 * chip + j // 8, 8 * k + j % 8)

    swaps = [
        remote(cp_hbm, cpin, swap_send.at[0], swap_recv.at[0], mate, o),
        remote(vp_hbm, vp.at[:, own], swap_send.at[1], swap_recv.at[1], mate, o),
    ]
    written = []
    done = set()

    def once(name):
        new = name not in done
        done.add(name)
        return new

    def send(*copy):
        remote(*copy).start()

    def encode_own(half, group):
        row = 1024 * lax.div(group, 2) + 512 * half + 256 * lax.rem(group, 2)
        eh[...], el[...] = two_terms(x[pl.ds(pl.multiple_of(row, 256), 256), :])

        def tile(n, carry):
            columns = pl.ds(pl.multiple_of(1024 * k + 512 * n, 512), 512)
            prod = product(eh[...], el[...], ch[:, columns], cl[:, columns], 0)
            prod = prod.reshape(8, 32, 512) * vp[:, columns][None]
            part0[
                half, pl.ds(pl.multiple_of(8 * group, 8), 8), pl.ds(pl.multiple_of(512 * n, 512), 512)
            ] = jnp.sum(prod, axis=1)
            return carry

        lax.fori_loop(0, 2, tile, 0)

    def encode_chunk(chunk):
        eh[...], el[...] = two_terms(first[chunk * CHUNK : (chunk + 1) * CHUNK, :])

        def tile(n, carry):
            columns = pl.ds(pl.multiple_of(512 * n, 512), 512)
            prod = product(eh[...], el[...], ch[:, columns], cl[:, columns], 0)
            prod = prod.reshape(8, 32, 512) * vp[:, columns][None]
            row = 8 * (chunk % 2)
            part1[chunk // 2, row : row + 8, columns] = jnp.sum(prod, axis=1)
            return carry

        lax.fori_loop(0, 4, tile, 0)

    def decode_chunk(chunk, app):
        def weigh(j, carry):
            rows = pl.ds(pl.multiple_of(32 * j, 32), 32)
            h, l = two_terms(vp[...] * inter[app, chunk // 2, pl.ds(8 * (chunk % 2) + j, 1), :])
            dh[rows, :] = h
            dl[rows, :] = l
            return carry

        lax.fori_loop(0, 8, weigh, 0)
        kout[app, chunk * CHUNK : (chunk + 1) * CHUNK, :] = product(dh[...], dl[...], ch[...], cl[...], 1)

    def exchange(app, half):
        sem = lambda i: (flat_send.at[app, half, i], flat_recv.at[app, half, i])
        g1, g2, g3, one = (
            (r.at[half] for r in ((got1b, got2b, got3b, piece1b) if app else (got1, got2, got3, piece1)))
        )
        if app:
            for d in FARTHEST:
                t = lax.rem(p + d, PTS)
                for h in range(2):
                    source = part1.at[
                        half,
                        pl.ds(pl.multiple_of(8 * lax.div(t, 8), 8), 8),
                        pl.ds(pl.multiple_of(1024 * h + 128 * lax.rem(t, 8), 128), 128),
                    ]
                    target = g1.at[2 * chip + h, k]
                    if d == 0:
                        local(source, target, sem(0)[1]).start()
                    else:
                        send(source, target, *sem(0), t, o)
            yield 1.0, 5.0
        else:
            for j in range(4):
                group = lax.rem(px + j, 4)
                encode_own(half, group)
                if once("greeted"):
                    pl.semaphore_wait(barrier, 15 + 15 + 16)
                    for copy in swaps:
                        copy.start()
                for u in range(4):
                    t = 4 * group + lax.rem(p + u, 4)
                    source = part0.at[
                        half,
                        pl.ds(pl.multiple_of(8 * group, 8), 8),
                        pl.ds(pl.multiple_of(256 * lax.rem(p + u, 4), 256), 256),
                    ]
                    if j == 0 and u == 0:
                        local(source, g1.at[p], sem(0)[1]).start()
                    else:
                        send(source, g1.at[p], *sem(0), t, o)
                yield 1.6, 3.0 if j == 3 else 0.0
        arrived(g1, sem(0)[1])

        for d in FARTHEST:
            s = lax.rem(o + d, ORB)
            if d == 0:
                local(g1.at[o], g2.at[o], sem(1)[1]).start()
            else:
                send(g1.at[s], g2.at[o], *sem(1), p, s)
        if once("screened"):
            loads[2].wait()
            cut_rows(wbuf, whi, wlo)
        yield 0.8, 7.5
        arrived(g2, sem(1)[1])
        one[...] = total_of(g2)

        for d in FARTHEST:
            if d == 0:
                local(one, g3.at[p], sem(2)[1]).start()
            else:
                send(one, g3.at[p], *sem(2), lax.rem(p + d, PTS), o)
        yield 0.8, 5.0
        arrived(g3, sem(2)[1])
        for t in range(PTS):
            if app:
                for j in range(2):
                    row, column = 16 * j + 8 * (t // 8), 128 * (t % 8)
                    chosen[row : row + 8, column : column + 128] = g3[t, j]
            else:
                row, column = 8 * (t // 4), 256 * (t % 4)
                chosen[row : row + 8, column : column + 256] = g3[t]
        high, low = two_terms(chosen[...])
        both = jnp.concatenate([high, low], axis=0)
        assert "screened" in done
        for i in range(4):
            rows = slice(256 * i, 256 * i + 256)
            prod = times(both, whi[rows, :], 1)
            terms[app, half, :, rows] = prod[:32] + (prod[32:] + times(high, wlo[rows, :], 1))

        def share(s):
            return terms.at[
                app, half,
                pl.ds(pl.multiple_of(8 * lax.div(s, 4), 8), 8),
                pl.ds(pl.multiple_of(256 * lax.rem(s, 4), 256), 256),
            ]

        g4, two = got4.at[app, half], piece2.at[app, half]
        for d in FARTHEST:
            s = lax.rem(o + d, ORB)
            if d == 0:
                local(share(o), g4.at[o], sem(3)[1]).start()
            else:
                send(share(s), g4.at[o], *sem(3), p, s)
        yield 3.0, 7.5
        arrived(g4, sem(3)[1])
        two[...] = total_of(g4)

        target = inter.at[
            app, half,
            pl.ds(pl.multiple_of(8 * lax.rem(lax.div(o, 4), 2), 8), 8),
            pl.ds(pl.multiple_of(1024 * k + 256 * lax.rem(o, 4), 256), 256),
        ]
        for d in FARTHEST:
            copy = remote(two, target, *sem(4), 2 * chip + half5, lax.rem(o + d, ORB))
            if d == 0:
                @pl.when(self5)
                def _():
                    local(two, target, sem(4)[1]).start()
                    local(two, spare.at[app, half], sem(4)[0]).start()

                @pl.when(jnp.logical_not(self5))
                def _():
                    copy.start()
            else:
                copy.start()
        yield 0.8, 7.5
        arrived(inter.at[app, half], sem(4)[1])

    def decode_and_reduce(app, half):
        result = last if app else first
        chunks = (2 * half, 2 * half + 1)

        def rows_of(ref, row, count):
            return ref.at[pl.ds(pl.multiple_of(row, 8), count), :]

        base, landing = {}, {}
        row = 448 * half
        for c in chunks:
            start = c * CHUNK
            for i in range(3):
                h = 8 * SHARES[c][i]
                lower = start
                for step in range(3):
                    size = h * (4 >> step)
                    base[c, i, step, "lower"] = lower
                    lower = lower + coordinate[DIMS[i][step]] * size
                    base[c, i, step] = lower
                    landing[c, i, step] = row
                    row += size
                start += 8 * h
        flying = {}

        def halve(c, i, step):
            size = 8 * SHARES[c][i] * (4 >> step)
            away = base[c, i, step, "lower"] + (1 - coordinate[DIMS[i][step]]) * size
            flying[c, i] = remote(
                rows_of(acc.at[app] if step else kout.at[app], away, size),
                rows_of(got.at[app], landing[c, i, step], size),
                cube_send.at[app, half], cube_recv.at[app, c, i, step],
                partner[DIMS[i][step]], o,
            )
            flying[c, i].start()

        def spread(c, i, step):
            block = rows_of(result, base[c, i, step], 8 * SHARES[c][i] * (4 >> step))
            flying[c, i] = remote(
                block, block, cube_send.at[app, half], cube_recv.at[app, c, i, 3 + step],
                partner[DIMS[i][step]], o,
            )
            flying[c, i].start()

        def to_mate(row, size):
            if app:
                send(rows_of(result, row, size), rows_of(out_hbm.at[k], row, size), mate_send, mate_recv, mate, o)

        def advance(c, stage):
            for i in range(3):
                h = 8 * SHARES[c][i]
                if stage == 0:
                    halve(c, i, 0)
                    continue
                flying[c, i].wait_recv()
                if stage <= 3:
                    step = stage - 1
                    size = h * (4 >> step)
                    mine = base[c, i, step]
                    source = acc.at[app] if step else kout.at[app]
                    summed = rows_of(source, mine, size)[...] + rows_of(got.at[app], landing[c, i, step], size)[...]
                    if stage < 3:
                        rows_of(acc.at[app], mine, size)[...] = summed
                        halve(c, i, stage)
                    else:
                        gap = rows_of(gap_ref, lax.rem(mine, 32), h)[...]
                        start = rows_of(x, ROWS * k + mine, h)[...]
                        if app:
                            value = (summed + gap * rows_of(first, mine, h)[...]) - start
                        else:
                            value = 0.5 * (summed + gap * start)
                        rows_of(result, mine, h)[...] = value
                        spread(c, i, 2)
                        to_mate(mine, h)
                else:
                    step = 6 - stage
                    size = h * (4 >> step)
                    if step:
                        spread(c, i, step - 1)
                    to_mate(base[c, i, step, "lower"] + (1 - coordinate[DIMS[i][step]]) * size, size)

        if once("swapped"):
            for copy in swaps:
                copy.wait_recv()
            cut_rows(cpin, ch, cl, other)
        for wave in range(2 + 6):
            busy = 0.3
            for c in reversed(chunks):
                stage = wave - (c % 2)
                if stage == 0:
                    decode_chunk(c, app)
                    busy += 2.3
                if 0 <= stage <= 6:
                    advance(c, stage)
            if wave >= 6:
                c = chunks[wave - 6]
                if app:
                    chunk = pl.ds(c * CHUNK, CHUNK)
                    copy = local(last.at[chunk, :], out_hbm.at[k, chunk, :], last_sem.at[c])
                    copy.start()
                    written.append(copy)
                else:
                    encode_chunk(c)
                    busy += 2.8
            yield busy, (0.0 if wave in (0, 7) else WAIT[wave])

    def stream(half):
        for app in range(2):
            yield from exchange(app, half)
            yield from decode_and_reduce(app, half)

    for v in range(32):
        gap_ref[v : v + 1, :] = (ce_ref[...] - ve_ref[v]) - center_shift
    for i in (0, 3):
        loads[i].wait()
    cut_rows(cpown, ch, cl, own)
    loads[1].wait()

    streams = [stream(half) for half in range(2)]
    ready = {0: 0.0, 1: 0.0}
    clock = 0.0
    while ready:
        half = min(ready, key=lambda i: (max(ready[i], clock), i))
        clock = max(clock, ready[half])
        try:
            busy, delay = next(streams[half])
        except StopIteration:
            del ready[half]
            continue
        clock += busy
        ready[half] = clock + delay

    arrived(out_hbm.at[1 - k], mate_recv)
    for copy in written:
        copy.wait()
    for copy in swaps:
        copy.wait_send()
    for app in range(2):
        for half in range(2):
            pieces = got4.at[app, half]
            for i in range(4):
                arrived(pieces.at[: ORB - 1], flat_send.at[app, half, i])
            arrived(pieces, flat_send.at[app, half, 4])
            arrived(got.at[app], cube_send.at[app, half])
    arrived(last, mate_send)


WAIT = (0.0, 3.0, 2.5, 2.0, 2.0, 2.5, 3.0, 0.0)


def steps(amplitudes, conduction, valence, screened, lower, upper):
    dma = pltpu.SemaphoreType.DMA
    f32 = lambda *shape: pltpu.VMEM(shape, F32)
    b16 = lambda *shape: pltpu.VMEM(shape, BF16)
    return pl.pallas_call(
        kernel,
        out_shape=jax.ShapeDtypeStruct((2, ROWS, 512), F32),
        in_specs=[ANY, ANY, ANY, ANY, pl.BlockSpec(memory_space=pltpu.SMEM), VMEM],
        out_specs=ANY,
        scratch_shapes=[
            f32(2 * ROWS, 512),
            f32(512, 1024), f32(512, 1024),
            b16(512, 2048), b16(512, 2048),
            f32(32, 2048),
            f32(1024, 1024), b16(1024, 1024), b16(1024, 1024),
            f32(2, 32, 1024), f32(2, 16, 2048),
            f32(2, 16, 8, 256), f32(2, 16, 2, 8, 128),
            f32(2, 16, 8, 256), f32(2, 16, 2, 8, 128),
            f32(2, 8, 256), f32(2, 2, 8, 128),
            f32(2, 16, 8, 256), f32(2, 16, 2, 8, 128),
            f32(32, 1024), f32(2, 2, 32, 1024),
            f32(2, 2, 16, 8, 256), f32(2, 2, 8, 256), f32(2, 2, 8, 256),
            f32(2, 2, 16, 2048),
            b16(CHUNK, 512), b16(CHUNK, 512),
            b16(CHUNK, 2048), b16(CHUNK, 2048),
            f32(2, ROWS, 512), f32(2, ROWS, 512), f32(2, 7 * 128, 512),
            f32(ROWS, 512), f32(ROWS, 512), f32(32, 512),
            dma((4,)), dma((2,)), dma((2,)), dma((2, 2, 5)), dma((2, 2, 5)),
            dma((2, 2)), dma((2, CHUNKS, 3, 6)), dma((CHUNKS,)), dma, dma,
        ],
        compiler_params=pltpu.CompilerParams(collective_id=0, has_side_effects=True),
        name="steps",
    )(amplitudes, conduction, valence, screened, lower, upper)


def body(
    amplitudes, valence_points, conduction_points, screened, valence_energy, conduction_energy
):
    flat = amplitudes.reshape(2 * ROWS, amplitudes.shape[2])
    second = steps(
        flat, conduction_points, valence_points, screened, valence_energy, conduction_energy[None, :]
    )
    return second.reshape(amplitudes.shape)


def solution(mesh):
    return jax.shard_map(
        body,
        mesh=mesh,
        in_specs=(
            P(None, "orb", None),
            P("orb", "pts"),
            P(None, "pts"),
            P("pts", "orb"),
            P("orb"),
            P(),
        ),
        out_specs=P(None, "orb", None),
        check_vma=False,
    )
```
